32 devices in a mesh: groups: 2 (over x), seq: 16 (over z, y, core).
Axes of the slice: x: 2, y: 2, z: 4, core: 2. Of those that a mesh axis runs over, the one named last changes fastest.
Arguments:
- queries: bfloat16 [8192, 1024], P(('groups', 'seq')), parts along dimension 0, may hold values from -6 to 6
- keys: bfloat16 [8192, 1024], P(('groups', 'seq')), parts along dimension 0, may hold values from -6 to 6
- values: bfloat16 [8192, 1024], P(('groups', 'seq')), parts along dimension 0, may hold values from -6 to 6
- grad_out: bfloat16 [8192, 1024], P(('groups', 'seq')), parts along dimension 0, may hold values from -0.0078125 to 0.0078125
Outputs:
- grad_queries: bfloat16 [1024, 8192], P('seq', 'groups'), parts along dimension 1
- grad_keys: bfloat16 [1024, 8192], P('seq', 'groups'), parts along dimension 1
- grad_values: bfloat16 [1024, 8192], P('seq', 'groups'), parts along dimension 1
The draws below stay inside these ranges and needn't reach their ends.
There are 2 independent parts, one for each index of `groups`. The reference program is written for one: setup_inputs(seed, part) draws one part's arguments, and reference() takes and returns one part's arrays. A program takes and returns all parts, laid end to end along the dimension named above; each array names one. Nothing has to cross between parts.
All inputs are finite; a program needn't handle non-finite values.
Results may differ from the reference program's by a relative error of at most 0.005.
Values may be sent and summed in bfloat16 or wider, within the bound.
No kernel may reach another device: no remote copies, remote signals or barrier semaphores. Data moves between devices by JAX's collectives and lax.ppermute only.
A program may use at most 256 MiB of HBM per device.

```python
import jax
import jax.numpy as jnp
from jax import lax

HEADS = 8
HDIM = 128
TOK_DEV = 256
D = 1024
TOKENS = 4096


def steps_of(stream_key, dims, cuts, low, high):
    loudness, own = 1.0, jax.random.fold_in(stream_key, 6)
    for axis_at, shards_of in cuts:
        draws = jnp.exp(jax.random.uniform(jax.random.fold_in(own, axis_at), (shards_of,), jnp.float32, low / len(cuts), high / len(cuts)))
        loudness = loudness * jnp.repeat(draws, dims[axis_at] // shards_of).reshape([-1 if axis == axis_at else 1 for axis in range(len(dims))])
    return loudness


def noise(own_key, dims, scale, bound, cuts=(), kind=jnp.bfloat16):
    drawn = jax.random.normal(own_key, dims, jnp.float32) * scale
    if len(cuts) > 0:
        drawn = steps_of(own_key, dims, cuts, -0.22, 0.18) * drawn
    return jnp.clip(drawn, min=-bound, max=bound).astype(kind)


def setup_inputs(seed: int = 0, part: int = 0) -> dict:
    arg_keys = jax.random.split(jax.random.key(seed), 5)
    own_keys = jax.random.split(jax.random.fold_in(arg_keys[4], part), 5)
    queries = noise(own_keys[0], (TOKENS, D), 1.0, 6.0, ((0, 16),))
    keys = noise(own_keys[1], (TOKENS, D), 1.0, 6.0, ((0, 16),))
    values = noise(own_keys[2], (TOKENS, D), 1.0, 6.0, ((0, 16),))
    grad_out = noise(own_keys[3], (TOKENS, D), (HDIM * TOKENS) ** -0.5, 0.0078125, ((0, 16),))
    return {"queries": queries, "keys": keys, "values": values, "grad_out": grad_out}


def block_states(pieces):
    query_segment, key_segment, value_segment, gradient_segment = pieces
    state_segment = jnp.einsum('anx,ane->nxe', key_segment.astype(jnp.float32), value_segment.astype(jnp.float32))
    state_gradient = jnp.einsum('orf,orb->rfb', query_segment.astype(jnp.float32), gradient_segment.astype(jnp.float32))
    return state_segment, state_gradient


def block_gradients(pieces):
    query_segment, key_segment, value_segment, gradient_segment, before_part, after_part = pieces
    query32 = query_segment.astype(jnp.float32)
    key_float32 = key_segment.astype(jnp.float32)
    value32 = value_segment.astype(jnp.float32)
    gradient_float32 = gradient_segment.astype(jnp.float32)
    positions = jnp.arange(TOK_DEV, dtype=jnp.int32)
    causal = positions[:, None] >= positions[None, :]
    scores_qk = jnp.einsum('thd,shd->hts', query32, key_float32)
    scores_gv = jnp.einsum('thd,shd->hts', gradient_float32, value32)
    masked_query_key = lax.optimization_barrier(jnp.where(causal[None], scores_qk, 0.0).astype(jnp.bfloat16)).astype(jnp.float32)
    masked_gv = lax.optimization_barrier(jnp.where(causal[None], scores_gv, 0.0).astype(jnp.bfloat16)).astype(jnp.float32)
    state_half = lax.optimization_barrier(before_part.astype(jnp.bfloat16)).astype(jnp.float32)
    gradient_halves = lax.optimization_barrier(after_part.astype(jnp.bfloat16)).astype(jnp.float32)
    grad_query = jnp.einsum('shd,hts->hdt', key_float32, masked_gv) + jnp.einsum('hdv,thv->hdt', state_half, gradient_float32)
    grad_key = jnp.einsum('thd,hts->hds', query32, masked_gv) + jnp.einsum('hdv,shv->hds', gradient_halves, value32)
    value_gradient = jnp.einsum('aci,cad->cid', gradient_float32, masked_query_key) + jnp.einsum('ioj,zio->ijz', gradient_halves, key_float32)
    stacked = jnp.stack([grad_query, grad_key, value_gradient]).reshape(3, HEADS * HDIM, TOK_DEV)
    return stacked.astype(jnp.bfloat16)


def reference(queries, keys, values, grad_out):
    blocks = TOKENS // TOK_DEV
    shaped = [arr.reshape(blocks, TOK_DEV, HEADS, HDIM) for arr in (queries, keys, values, grad_out)]
    state_own, grad_own = lax.map(block_states, tuple(shaped))
    state_before = jnp.cumsum(state_own, axis=0) - state_own
    grad_totals = jnp.sum(grad_own, axis=0)
    grad_after = grad_totals[None] - jnp.cumsum(grad_own, axis=0)
    gradients = lax.map(block_gradients, (shaped[0], shaped[1], shaped[2], shaped[3], state_before, grad_after))
    merged = jnp.transpose(gradients, (1, 2, 0, 3)).reshape(3, HEADS * HDIM, TOKENS)
    return (merged[0], merged[1], merged[2])
```

```python
import functools

import jax
import jax.numpy as jnp
from jax import lax
from jax.experimental import pallas as pl
from jax.experimental.pallas import tpu as pltpu
from jax.sharding import PartitionSpec as P

HDIM = 128
CORES = 2


def dot(a, b, contract):
    return lax.dot_general(a, b, (contract, ((), ())), preferred_element_type=jnp.float32)


NN = ((1,), (0,))
NT = ((1,), (1,))
TN = ((0,), (0,))


def entering(shard, axis, reverse):
    size, position = lax.axis_size(axis), lax.axis_index(axis)
    everything = lax.all_gather(shard, axis)
    start = jnp.zeros_like(shard)

    def lap(k, before):
        at = size - 1 - k if reverse else k
        reached = at > position if reverse else at < position
        return jnp.where(reached, before + everything[at], before)

    return lax.fori_loop(0, size, lap, start)


def general_body(queries, keys, values, grad_out):
    length = queries.shape[0]
    head_count = queries.shape[1] // HDIM
    split = lambda x: jnp.transpose(x.reshape(length, head_count, HDIM), (1, 0, 2))
    q, k, v, g = split(queries), split(keys), split(values), split(grad_out)
    einsum = functools.partial(jnp.einsum, preferred_element_type=jnp.float32)
    positions = lax.iota(jnp.int32, length)
    causal = positions[:, None] >= positions[None, :]
    scores_qk = jnp.where(causal[None], einsum("htd,hsd->hts", q, k), 0.0).astype(jnp.bfloat16)
    scores_gv = jnp.where(causal[None], einsum("htd,hsd->hts", g, v), 0.0).astype(jnp.bfloat16)
    state_half = entering(einsum("hsd,hse->hde", k, v), "seq", False).astype(jnp.bfloat16)
    grad_half = entering(einsum("htf,htb->hfb", q, g), "seq", True).astype(jnp.bfloat16)
    grad_q = einsum("hsd,hts->hdt", k, scores_gv) + einsum("hdv,htv->hdt", state_half, g)
    grad_k = einsum("htd,hts->hds", q, scores_gv) + einsum("hdv,hsv->hds", grad_half, v)
    grad_v = einsum("htd,hts->hds", g, scores_qk) + einsum("hfb,hsf->hbs", grad_half, k)
    width = head_count * HDIM
    rows = [x.reshape(width, length).astype(jnp.bfloat16) for x in (grad_q, grad_k, grad_v)]
    return tuple(lax.all_to_all(x, "seq", split_axis=0, concat_axis=1, tiled=True) for x in rows)


def pack_kernel(flips, tensors, meta, *refs):
    ins, outs, sems = refs[:tensors], refs[tensors:-1], refs[-1]
    copies = []
    for i, flip in enumerate(flips):
        head = meta[0] ^ flip
        for t in range(tensors):
            columns = pl.ds(pl.multiple_of(head * HDIM, HDIM), HDIM)
            copies.append(
                pltpu.make_async_copy(ins[t].at[:, columns], outs[i].at[t], sems.at[i, t])
            )
    for copy in copies:
        copy.start()
    for copy in copies:
        copy.wait()


def pack(meta, flips, arrays):
    length, tensors = arrays[0].shape[0], len(arrays)
    shape = jax.ShapeDtypeStruct((tensors, length, HDIM), arrays[0].dtype)
    any_spec = pl.BlockSpec(memory_space=pl.ANY)
    return pl.pallas_call(
        functools.partial(pack_kernel, flips, tensors),
        out_shape=[shape] * len(flips),
        in_specs=[pl.BlockSpec(memory_space=pltpu.SMEM)] + [any_spec] * tensors,
        out_specs=[any_spec] * len(flips),
        scratch_shapes=[pltpu.SemaphoreType.DMA((len(flips), tensors))],
    )(meta, *arrays)


def attend_kernel(chips, length, meta, *refs):
    n_blocks = chips * CORES
    blocks = refs[:n_blocks]
    out_q, out_k, out_v = refs[n_blocks : n_blocks + 3]
    states, grads, state_half, grad_half, intra, turned = refs[n_blocks + 3 :]
    chip, core = meta[0], meta[1]
    half = HDIM // CORES
    own_rows = pl.ds(pl.multiple_of(core * half, half), half)
    row = lax.broadcasted_iota(jnp.int32, (length, length), 0)
    column = lax.broadcasted_iota(jnp.int32, (length, length), 1)
    causal = row >= column

    def block_of(slot):
        flip, other = slot // CORES, slot % CORES
        return (chip ^ flip) * CORES + (core ^ other)

    for slot in range(n_blocks):
        at = block_of(slot)
        q, k, v, g = (blocks[slot][t] for t in range(4))
        scores_gv = jnp.where(causal, dot(g, v, NT), 0.0).astype(jnp.bfloat16)
        scores_qk = jnp.where(causal, dot(q, k, NT), 0.0).astype(jnp.bfloat16)
        turned[0] = k.T
        turned[1] = q.T
        turned[2] = g.T
        states[at] = dot(turned[0], v, NN)
        grads[at] = dot(turned[1], g, NN)
        intra[slot, 0] = dot(turned[0, own_rows, :], scores_gv, NT)
        intra[slot, 1] = dot(turned[1, own_rows, :], scores_gv, NN)
        intra[slot, 2] = dot(turned[2, own_rows, :], scores_qk, NN)

    total = jnp.zeros((HDIM, HDIM), jnp.float32)
    for b in range(n_blocks):
        state_half[b] = total.astype(jnp.bfloat16)
        total = total + states[b]
    total = jnp.zeros((HDIM, HDIM), jnp.float32)
    for b in reversed(range(n_blocks)):
        grad_half[b, 0] = total.astype(jnp.bfloat16)
        grad_half[b, 1] = total.T.astype(jnp.bfloat16)
        total = total + grads[b]

    for slot in range(n_blocks):
        at = block_of(slot)
        k, v, g = (blocks[slot][t] for t in range(1, 4))
        columns = pl.ds(pl.multiple_of(at * length, length), length)
        out_q[:, columns] = (
            intra[slot, 0] + dot(state_half[at, own_rows, :], g, NT)
        ).astype(out_q.dtype)
        out_k[:, columns] = (
            intra[slot, 1] + dot(grad_half[at, 0, own_rows, :], v, NT)
        ).astype(out_k.dtype)
        out_v[:, columns] = (
            intra[slot, 2] + dot(grad_half[at, 1, own_rows, :], k, NT)
        ).astype(out_v.dtype)


def attend(meta, blocks):
    n_blocks = len(blocks)
    length = blocks[0].shape[1]
    half = HDIM // CORES
    vmem = pl.BlockSpec(memory_space=pltpu.VMEM)
    out = jax.ShapeDtypeStruct((half, n_blocks * length), jnp.bfloat16)
    square = (n_blocks, HDIM, HDIM)
    return pl.pallas_call(
        functools.partial(attend_kernel, n_blocks // CORES, length),
        out_shape=[out] * 3,
        in_specs=[pl.BlockSpec(memory_space=pltpu.SMEM)] + [vmem] * n_blocks,
        out_specs=[vmem] * 3,
        scratch_shapes=[
            pltpu.VMEM(square, jnp.float32),
            pltpu.VMEM(square, jnp.float32),
            pltpu.VMEM(square, jnp.bfloat16),
            pltpu.VMEM((n_blocks, 2, HDIM, HDIM), jnp.bfloat16),
            pltpu.VMEM((n_blocks, 3, half, length), jnp.float32),
            pltpu.VMEM((3, HDIM, length), jnp.bfloat16),
        ],
        compiler_params=pltpu.CompilerParams(vmem_limit_bytes=40 * 1024 * 1024),
    )(meta, *blocks)


def chip_body(queries, keys, values, grad_out):
    size, position = lax.axis_size("seq"), lax.axis_index("seq")
    chips = size // CORES
    meta = jnp.stack([position // CORES, position % CORES]).astype(jnp.int32)
    arrays = (queries, keys, values, grad_out)
    order = sorted(range(chips), reverse=True)
    packed = dict(zip(order, pack(meta, order, arrays)))
    flipped = lambda x, flip: lax.ppermute(x, "seq", [(i, i ^ flip) for i in range(size)])
    blocks = {}
    for flip in order:
        mine = flipped(packed[flip], flip * CORES) if flip else packed[flip]
        blocks[flip] = (mine, flipped(mine, 1))
    return tuple(attend(meta, [x for flip in range(chips) for x in blocks[flip]]))


def solution(mesh):
    in_specs = (P(("groups", "seq"), None),) * 4
    out_specs = (P("seq", "groups"),) * 3

    def body(queries, keys, values, grad_out):
        heads = queries.shape[1] // HDIM
        chosen = chip_body if mesh.shape["seq"] == heads * CORES else general_body
        return chosen(queries, keys, values, grad_out)

    return jax.shard_map(body, mesh=mesh, in_specs=in_specs, out_specs=out_specs, check_vma=False)
```

```python
import functools

import jax
import jax.numpy as jnp
from jax import lax
from jax.experimental import pallas as pl
from jax.experimental.pallas import tpu as pltpu
from jax.sharding import PartitionSpec as P

HDIM = 128
CORES = 2


def dot(a, b, contract):
    return lax.dot_general(a, b, (contract, ((), ())), preferred_element_type=jnp.float32)


NN = ((1,), (0,))
NT = ((1,), (1,))
TN = ((0,), (0,))


def entering(shard, axis, reverse):
    size, position = lax.axis_size(axis), lax.axis_index(axis)
    everything = lax.all_gather(shard, axis)
    start = jnp.zeros_like(shard)

    def lap(k, before):
        at = size - 1 - k if reverse else k
        reached = at > position if reverse else at < position
        return jnp.where(reached, before + everything[at], before)

    return lax.fori_loop(0, size, lap, start)


def general_body(queries, keys, values, grad_out):
    length = queries.shape[0]
    head_count = queries.shape[1] // HDIM
    split = lambda x: jnp.transpose(x.reshape(length, head_count, HDIM), (1, 0, 2))
    q, k, v, g = split(queries), split(keys), split(values), split(grad_out)
    einsum = functools.partial(jnp.einsum, preferred_element_type=jnp.float32)
    positions = lax.iota(jnp.int32, length)
    causal = positions[:, None] >= positions[None, :]
    scores_qk = jnp.where(causal[None], einsum("htd,hsd->hts", q, k), 0.0).astype(jnp.bfloat16)
    scores_gv = jnp.where(causal[None], einsum("htd,hsd->hts", g, v), 0.0).astype(jnp.bfloat16)
    state_half = entering(einsum("hsd,hse->hde", k, v), "seq", False).astype(jnp.bfloat16)
    grad_half = entering(einsum("htf,htb->hfb", q, g), "seq", True).astype(jnp.bfloat16)
    grad_q = einsum("hsd,hts->hdt", k, scores_gv) + einsum("hdv,htv->hdt", state_half, g)
    grad_k = einsum("htd,hts->hds", q, scores_gv) + einsum("hdv,hsv->hds", grad_half, v)
    grad_v = einsum("htd,hts->hds", g, scores_qk) + einsum("hfb,hsf->hbs", grad_half, k)
    width = head_count * HDIM
    rows = [x.reshape(width, length).astype(jnp.bfloat16) for x in (grad_q, grad_k, grad_v)]
    return tuple(lax.all_to_all(x, "seq", split_axis=0, concat_axis=1, tiled=True) for x in rows)


def place():
    position = lax.axis_index("seq")
    return position // CORES, position % CORES


SMALL = pl.CostEstimate(flops=1, transcendentals=0, bytes_accessed=1)


def pack_kernel(flips, tensors, *refs):
    ins, outs, sems = refs[:tensors], refs[tensors:-1], refs[-1]
    chip, _ = place()
    copies = []
    for i, flip in enumerate(flips):
        columns = pl.ds(pl.multiple_of((chip ^ flip) * HDIM, HDIM), HDIM)
        for t in range(tensors):
            copies.append(
                pltpu.make_async_copy(ins[t].at[:, columns], outs[i].at[t], sems.at[i, t])
            )
    for copy in copies:
        copy.start()
    for copy in copies:
        copy.wait()


def pack(flips, arrays):
    length, tensors = arrays[0].shape[0], len(arrays)
    shape = pltpu.VMEM((tensors, length, HDIM), arrays[0].dtype)
    return pl.pallas_call(
        functools.partial(pack_kernel, flips, tensors),
        out_shape=[shape] * len(flips),
        in_specs=[pl.BlockSpec(memory_space=pl.ANY)] * tensors,
        out_specs=[pl.BlockSpec(memory_space=pltpu.VMEM)] * len(flips),
        scratch_shapes=[pltpu.SemaphoreType.DMA((len(flips), tensors))],
        cost_estimate=SMALL,
    )(*arrays)


def within_blocks(blocks, core, turned, states, grads, intra):
    length = blocks[0].shape[1]
    half = HDIM // CORES
    own_rows = pl.ds(pl.multiple_of(core * half, half), half)
    row = lax.broadcasted_iota(jnp.int32, (length, length), 0)
    column = lax.broadcasted_iota(jnp.int32, (length, length), 1)
    causal = row >= column
    for i, block in enumerate(blocks):
        q, k, v, g = (block[t] for t in range(4))
        scores_gv = jnp.where(causal, dot(g, v, NT), 0.0).astype(jnp.bfloat16)
        scores_qk = jnp.where(causal, dot(q, k, NT), 0.0).astype(jnp.bfloat16)
        turned[i, 0] = k.T
        turned[i, 1] = q.T
        turned[i, 2] = g.T
        states[i] = dot(turned[i, 0], v, NN)
        grads[i] = dot(turned[i, 1], g, NN)
        intra[i, 0] = dot(turned[i, 0, own_rows, :], scores_gv, NT)
        intra[i, 1] = dot(turned[i, 1, own_rows, :], scores_gv, NN)
        intra[i, 2] = dot(turned[i, 2, own_rows, :], scores_qk, NN)


def within_shapes(count, length):
    return [
        ((count, HDIM, HDIM), jnp.float32),
        ((count, HDIM, HDIM), jnp.float32),
        ((count, 3, HDIM // CORES, length), jnp.float32),
    ]


def turned_scratch(count, length):
    return pltpu.VMEM((count, 3, HDIM, length), jnp.bfloat16)


VMEM_SPEC = pl.BlockSpec(memory_space=pltpu.VMEM)
PARAMS = pltpu.CompilerParams(vmem_limit_bytes=40 * 1024 * 1024)


def within_kernel(count, *refs):
    _, core = place()
    within_blocks(refs[:count], core, refs[-1], *refs[count:-1])


def within(blocks):
    count, length = len(blocks), blocks[0].shape[1]
    return pl.pallas_call(
        functools.partial(within_kernel, count),
        out_shape=[jax.ShapeDtypeStruct(*s) for s in within_shapes(count, length)],
        in_specs=[VMEM_SPEC] * count,
        out_specs=[VMEM_SPEC] * 3,
        scratch_shapes=[turned_scratch(count, length)],
        cost_estimate=SMALL,
        compiler_params=PARAMS,
    )(*blocks)


def finish_kernel(flips, sizes, *refs):
    n_blocks = sum(sizes)
    blocks = refs[:n_blocks]
    done = [refs[n_blocks + 3 * i : n_blocks + 3 * i + 3] for i in range(len(sizes) - 1)]
    at = n_blocks + 3 * len(done)
    outs, (state_half, grad_half, in_order), last, turned = (
        refs[at : at + 3],
        refs[at + 3 : at + 6],
        refs[at + 6 : at + 9],
        refs[at + 9],
    )
    chip, core = place()
    half, length = HDIM // CORES, blocks[0].shape[1]
    own_rows = pl.ds(pl.multiple_of(core * half, half), half)
    within_blocks(blocks[n_blocks - sizes[-1] :], core, turned, *last)
    done.append(last)

    slots = []
    for size, (states, grads, intra) in zip(sizes, done):
        for i in range(size):
            slot = len(slots)
            b = (chip ^ flips[slot // CORES]) * CORES + (core ^ (slot % CORES))
            in_order[b, 0] = states[i]
            in_order[b, 1] = grads[i]
            slots.append((b, intra.at[i]))

    total = jnp.zeros((HDIM, HDIM), jnp.float32)
    for b in range(n_blocks):
        state_half[b] = total.astype(jnp.bfloat16)
        total = total + in_order[b, 0]
    total = jnp.zeros((HDIM, HDIM), jnp.float32)
    for b in reversed(range(n_blocks)):
        grad_half[b, 0] = total.astype(jnp.bfloat16)
        grad_half[b, 1] = total.T.astype(jnp.bfloat16)
        total = total + in_order[b, 1]

    for block, (b, intra) in zip(blocks, slots):
        k, v, g = (block[t] for t in range(1, 4))
        columns = pl.ds(pl.multiple_of(b * length, length), length)
        across = (
            dot(state_half[b, own_rows, :], g, NT),
            dot(grad_half[b, 0, own_rows, :], v, NT),
            dot(grad_half[b, 1, own_rows, :], k, NT),
        )
        for j, out in enumerate(outs):
            out[:, columns] = (intra[j] + across[j]).astype(out.dtype)


def finish(flips, blocks, done, sizes):
    n_blocks, length = len(blocks), blocks[0].shape[1]
    half = HDIM // CORES
    out = jax.ShapeDtypeStruct((half, n_blocks * length), jnp.bfloat16)
    return pl.pallas_call(
        functools.partial(finish_kernel, flips, sizes),
        out_shape=[out] * 3,
        in_specs=[VMEM_SPEC] * (n_blocks + len(done)),
        out_specs=[VMEM_SPEC] * 3,
        scratch_shapes=[
            pltpu.VMEM((n_blocks, HDIM, HDIM), jnp.bfloat16),
            pltpu.VMEM((n_blocks, 2, HDIM, HDIM), jnp.bfloat16),
            pltpu.VMEM((n_blocks, 2, HDIM, HDIM), jnp.float32),
        ]
        + [pltpu.VMEM(*s) for s in within_shapes(sizes[-1], length)]
        + [turned_scratch(sizes[-1], length)],
        compiler_params=PARAMS,
    )(*blocks, *done)


def after(x, *others):
    return lax.optimization_barrier((x, *others))[0]


def chip_body(queries, keys, values, grad_out):
    size = lax.axis_size("seq")
    chips = size // CORES
    arrays = (queries, keys, values, grad_out)
    near, far = list(range(chips // 2)), list(range(chips // 2, chips))[::-1]
    packed = dict(zip(far, pack(far, arrays))) | dict(zip(near, pack(near, arrays)))
    flipped = lambda x, flip: lax.ppermute(x, "seq", [(i, i ^ flip) for i in range(size)])
    order = [flip for pair in zip(far, near[1:] + [0]) for flip in pair]
    order.remove(0)
    held, before = {0: packed[0]}, []
    for flip in order:
        held[flip] = flipped(packed[flip], flip * CORES)
        held[flip] = after(held[flip], *before)
        before = [held[flip]]
    groups = (near, far[:-1], far[-1:])
    done, sizes, blocks = [], [], []
    for group in groups:
        some = []
        for flip in group:
            mine = after(held[flip], *done)
            some += [mine, flipped(mine, 1)]
        blocks += some
        sizes.append(len(some))
        if group is not groups[-1]:
            done += within(some)
    flips = [flip for group in groups for flip in group]
    return tuple(finish(flips, blocks, done, tuple(sizes)))


def solution(mesh):
    in_specs = (P(("groups", "seq"), None),) * 4
    out_specs = (P("seq", "groups"),) * 3

    def body(queries, keys, values, grad_out):
        heads = queries.shape[1] // HDIM
        chosen = chip_body if mesh.shape["seq"] == heads * CORES else general_body
        return chosen(queries, keys, values, grad_out)

    return jax.shard_map(body, mesh=mesh, in_specs=in_specs, out_specs=out_specs, check_vma=False)
```

```python
import functools

import jax
import jax.numpy as jnp
from jax import lax
from jax.experimental import pallas as pl
from jax.experimental.pallas import tpu as pltpu
from jax.sharding import PartitionSpec as P

HDIM = 128
CORES = 2


def dot(a, b, contract):
    return lax.dot_general(a, b, (contract, ((), ())), preferred_element_type=jnp.float32)


NN = ((1,), (0,))
NT = ((1,), (1,))
TN = ((0,), (0,))


def entering(shard, axis, reverse):
    size, position = lax.axis_size(axis), lax.axis_index(axis)
    everything = lax.all_gather(shard, axis)
    start = jnp.zeros_like(shard)

    def lap(k, before):
        at = size - 1 - k if reverse else k
        reached = at > position if reverse else at < position
        return jnp.where(reached, before + everything[at], before)

    return lax.fori_loop(0, size, lap, start)


def general_body(queries, keys, values, grad_out):
    length = queries.shape[0]
    head_count = queries.shape[1] // HDIM
    split = lambda x: jnp.transpose(x.reshape(length, head_count, HDIM), (1, 0, 2))
    q, k, v, g = split(queries), split(keys), split(values), split(grad_out)
    einsum = functools.partial(jnp.einsum, preferred_element_type=jnp.float32)
    positions = lax.iota(jnp.int32, length)
    causal = positions[:, None] >= positions[None, :]
    scores_qk = jnp.where(causal[None], einsum("htd,hsd->hts", q, k), 0.0).astype(jnp.bfloat16)
    scores_gv = jnp.where(causal[None], einsum("htd,hsd->hts", g, v), 0.0).astype(jnp.bfloat16)
    state_half = entering(einsum("hsd,hse->hde", k, v), "seq", False).astype(jnp.bfloat16)
    grad_half = entering(einsum("htf,htb->hfb", q, g), "seq", True).astype(jnp.bfloat16)
    grad_q = einsum("hsd,hts->hdt", k, scores_gv) + einsum("hdv,htv->hdt", state_half, g)
    grad_k = einsum("htd,hts->hds", q, scores_gv) + einsum("hdv,hsv->hds", grad_half, v)
    grad_v = einsum("htd,hts->hds", g, scores_qk) + einsum("hfb,hsf->hbs", grad_half, k)
    width = head_count * HDIM
    rows = [x.reshape(width, length).astype(jnp.bfloat16) for x in (grad_q, grad_k, grad_v)]
    return tuple(lax.all_to_all(x, "seq", split_axis=0, concat_axis=1, tiled=True) for x in rows)


CHIPS = 8
OWN, NEAR, FAR = 0, (1, 2, 3), (7, 6, 5, 4)
ISSUED = (7, 1, 6, 2, 5, 3, 4)
RELAYS = ((0, 1, 2), (3, 7, 6), (5, 4))
TENSORS = 4
VMEM_SPEC = pl.BlockSpec(memory_space=pltpu.VMEM)
PARAMS = pltpu.CompilerParams(vmem_limit_bytes=40 * 1024 * 1024)
SMALL = pl.CostEstimate(flops=1, transcendentals=0, bytes_accessed=1)


def place():
    position = lax.axis_index("seq")
    return position // CORES, position % CORES


def after(x, *others):
    return lax.optimization_barrier((x, *others))[0]


def pack_kernel(flips, *refs):
    ins, outs, sems = refs[:TENSORS], refs[TENSORS:-1], refs[-1]
    chip, _ = place()
    copies = []
    for i, flip in enumerate(flips):
        columns = pl.ds(pl.multiple_of((chip ^ flip) * HDIM, HDIM), HDIM)
        for t in range(TENSORS):
            copies.append(
                pltpu.make_async_copy(ins[t].at[:, columns], outs[i].at[t], sems.at[i, t])
            )
    for copy in copies:
        copy.start()
    for copy in copies:
        copy.wait()


def pack(flips, arrays):
    shape = pltpu.VMEM((TENSORS, arrays[0].shape[0], HDIM), arrays[0].dtype)
    packed = pl.pallas_call(
        functools.partial(pack_kernel, flips),
        out_shape=[shape] * len(flips),
        in_specs=[pl.BlockSpec(memory_space=pl.ANY)] * TENSORS,
        out_specs=[VMEM_SPEC] * len(flips),
        scratch_shapes=[pltpu.SemaphoreType.DMA((len(flips), TENSORS))],
        cost_estimate=SMALL,
    )(*arrays)
    return dict(zip(flips, packed))


def within_blocks(blocks, core, turned, states, grads, intra):
    length = turned.shape[-1]
    half = HDIM // CORES
    own_rows = pl.ds(pl.multiple_of(core * half, half), half)
    row = lax.broadcasted_iota(jnp.int32, (length, length), 0)
    column = lax.broadcasted_iota(jnp.int32, (length, length), 1)
    causal = row >= column
    for i, block in enumerate(blocks):
        q, k, v, g = (block[t] for t in range(TENSORS))
        scores_gv = jnp.where(causal, dot(g, v, NT), 0.0).astype(jnp.bfloat16)
        scores_qk = jnp.where(causal, dot(q, k, NT), 0.0).astype(jnp.bfloat16)
        turned[i, 0] = k.T
        turned[i, 1] = q.T
        turned[i, 2] = g.T
        states[i] = dot(turned[i, 0], v, NN)
        grads[i] = dot(turned[i, 1], g, NN)
        intra[i, 0] = dot(turned[i, 0, own_rows, :], scores_gv, NT)
        intra[i, 1] = dot(turned[i, 1, own_rows, :], scores_gv, NN)
        intra[i, 2] = dot(turned[i, 2, own_rows, :], scores_qk, NN)


def within_shapes(count, length):
    return [
        ((count, HDIM, HDIM), jnp.float32),
        ((count, HDIM, HDIM), jnp.float32),
        ((count, 3, HDIM // CORES, length), jnp.float32),
    ]


def turned_scratch(count, length):
    return pltpu.VMEM((count, 3, HDIM, length), jnp.bfloat16)


def bind(where, refs):
    return [refs[array].at[pl.ds(at * TENSORS, TENSORS)] for array, at in where]


def within_kernel(where, n_arrays, *refs):
    _, core = place()
    within_blocks(bind(where, refs), core, refs[-1], *refs[n_arrays:-1])


def within(where, arrays):
    count, length = len(where), arrays[0].shape[1]
    return pl.pallas_call(
        functools.partial(within_kernel, where, len(arrays)),
        out_shape=[jax.ShapeDtypeStruct(*s) for s in within_shapes(count, length)],
        in_specs=[VMEM_SPEC] * len(arrays),
        out_specs=[VMEM_SPEC] * 3,
        scratch_shapes=[turned_scratch(count, length)],
        cost_estimate=SMALL,
        compiler_params=PARAMS,
    )(*arrays)


def finish_kernel(where, slots, sizes, n_arrays, *refs):
    n_blocks = sum(sizes)
    blocks = bind(where, refs)
    done = [refs[n_arrays + 3 * i : n_arrays + 3 * i + 3] for i in range(len(sizes) - 1)]
    rest = refs[n_arrays + 3 * len(done) :]
    outs, (state_half, grad_half, in_order), last, turned = rest[:3], rest[3:6], rest[6:9], rest[9]
    chip, core = place()
    half, length = HDIM // CORES, turned.shape[-1]
    own_rows = pl.ds(pl.multiple_of(core * half, half), half)
    within_blocks(blocks[n_blocks - sizes[-1] :], core, turned, *last)
    done.append(last)

    found = []
    for size, (states, grads, intra) in zip(sizes, done):
        for i in range(size):
            flip, other = slots[len(found)]
            b = (chip ^ flip) * CORES + (core ^ other)
            in_order[b, 0] = states[i]
            in_order[b, 1] = grads[i]
            found.append((b, intra.at[i]))

    total = jnp.zeros((HDIM, HDIM), jnp.float32)
    for b in range(n_blocks):
        state_half[b] = total.astype(jnp.bfloat16)
        total = total + in_order[b, 0]
    total = jnp.zeros((HDIM, HDIM), jnp.float32)
    for b in reversed(range(n_blocks)):
        grad_half[b, 0] = total.astype(jnp.bfloat16)
        grad_half[b, 1] = total.T.astype(jnp.bfloat16)
        total = total + in_order[b, 1]

    for block, (b, intra) in zip(blocks, found):
        k, v, g = (block[t] for t in range(1, TENSORS))
        columns = pl.ds(pl.multiple_of(b * length, length), length)
        across = (
            dot(state_half[b, own_rows, :], g, NT),
            dot(grad_half[b, 0, own_rows, :], v, NT),
            dot(grad_half[b, 1, own_rows, :], k, NT),
        )
        for j, out in enumerate(outs):
            out[:, columns] = (intra[j] + across[j]).astype(out.dtype)


def finish(where, slots, arrays, sizes, done):
    n_blocks, length = sum(sizes), arrays[0].shape[1]
    out = jax.ShapeDtypeStruct((HDIM // CORES, n_blocks * length), jnp.bfloat16)
    return pl.pallas_call(
        functools.partial(finish_kernel, where, slots, sizes, len(arrays)),
        out_shape=[out] * 3,
        in_specs=[VMEM_SPEC] * (len(arrays) + len(done)),
        out_specs=[VMEM_SPEC] * 3,
        scratch_shapes=[
            pltpu.VMEM((n_blocks, HDIM, HDIM), jnp.bfloat16),
            pltpu.VMEM((n_blocks, 2, HDIM, HDIM), jnp.bfloat16),
            pltpu.VMEM((n_blocks, 2, HDIM, HDIM), jnp.float32),
        ]
        + [pltpu.VMEM(*s) for s in within_shapes(sizes[-1], length)]
        + [turned_scratch(sizes[-1], length)],
        compiler_params=PARAMS,
    )(*arrays, *done)


def chip_body(queries, keys, values, grad_out):
    size = lax.axis_size("seq")
    given = (queries, keys, values, grad_out)
    packed = pack(FAR, given) | pack((OWN,) + NEAR, given)
    flipped = lambda x, flip: lax.ppermute(x, "seq", [(i, i ^ flip) for i in range(size)])
    mine, previous = {OWN: packed[OWN]}, ()
    for flip in ISSUED:
        mine[flip] = after(flipped(packed[flip], flip * CORES), *previous)
        previous = (mine[flip],)

    early = (OWN,) + NEAR + FAR[:-1]
    done = within(tuple((i, 0) for i in range(len(early))), [mine[flip] for flip in early])
    relayed = []
    for flips in RELAYS:
        held = [after(mine[flip], *done) if flips is RELAYS[-1] else mine[flip] for flip in flips]
        relayed.append(flipped(jnp.concatenate(held), 1))
    theirs = [(flip, j, at) for j, flips in enumerate(RELAYS) for at, flip in enumerate(flips)]
    soon, late = theirs[: -len(RELAYS[-1])], theirs[-len(RELAYS[-1]) :]
    done += within(tuple((j, at) for _, j, at in soon), relayed[:-1])

    own = early + FAR[-1:]
    arrays = [mine[flip] for flip in own] + relayed
    where = {(flip, 0): (i, 0) for i, flip in enumerate(own)}
    where |= {(flip, 1): (len(own) + j, at) for flip, j, at in theirs}
    slots = tuple((flip, 0) for flip in early) + tuple((flip, 1) for flip, _, _ in soon)
    slots += ((FAR[-1], 0),) + tuple((flip, 1) for flip, _, _ in late)
    sizes = (len(early), len(soon), 1 + len(late))
    return tuple(finish(tuple(where[slot] for slot in slots), slots, arrays, sizes, done))


def solution(mesh):
    in_specs = (P(("groups", "seq"), None),) * 4
    out_specs = (P("seq", "groups"),) * 3

    def body(queries, keys, values, grad_out):
        heads = queries.shape[1] // HDIM
        one_head_per_chip = heads == CHIPS and mesh.shape["seq"] == CHIPS * CORES
        chosen = chip_body if one_head_per_chip else general_body
        return chosen(queries, keys, values, grad_out)

    return jax.shard_map(body, mesh=mesh, in_specs=in_specs, out_specs=out_specs, check_vma=False)
```

```python
import functools

import jax
import jax.numpy as jnp
from jax import lax
from jax.experimental import pallas as pl
from jax.experimental.pallas import tpu as pltpu
from jax.sharding import PartitionSpec as P

HDIM = 128
CORES = 2


def dot(a, b, contract):
    return lax.dot_general(a, b, (contract, ((), ())), preferred_element_type=jnp.float32)


NN = ((1,), (0,))
NT = ((1,), (1,))
TN = ((0,), (0,))


def entering(shard, axis, reverse):
    size, position = lax.axis_size(axis), lax.axis_index(axis)
    everything = lax.all_gather(shard, axis)
    start = jnp.zeros_like(shard)

    def lap(k, before):
        at = size - 1 - k if reverse else k
        reached = at > position if reverse else at < position
        return jnp.where(reached, before + everything[at], before)

    return lax.fori_loop(0, size, lap, start)


def general_body(queries, keys, values, grad_out):
    length = queries.shape[0]
    head_count = queries.shape[1] // HDIM
    split = lambda x: jnp.transpose(x.reshape(length, head_count, HDIM), (1, 0, 2))
    q, k, v, g = split(queries), split(keys), split(values), split(grad_out)
    einsum = functools.partial(jnp.einsum, preferred_element_type=jnp.float32)
    positions = lax.iota(jnp.int32, length)
    causal = positions[:, None] >= positions[None, :]
    scores_qk = jnp.where(causal[None], einsum("htd,hsd->hts", q, k), 0.0).astype(jnp.bfloat16)
    scores_gv = jnp.where(causal[None], einsum("htd,hsd->hts", g, v), 0.0).astype(jnp.bfloat16)
    state_half = entering(einsum("hsd,hse->hde", k, v), "seq", False).astype(jnp.bfloat16)
    grad_half = entering(einsum("htf,htb->hfb", q, g), "seq", True).astype(jnp.bfloat16)
    grad_q = einsum("hsd,hts->hdt", k, scores_gv) + einsum("hdv,htv->hdt", state_half, g)
    grad_k = einsum("htd,hts->hds", q, scores_gv) + einsum("hdv,hsv->hds", grad_half, v)
    grad_v = einsum("htd,hts->hds", g, scores_qk) + einsum("hfb,hsf->hbs", grad_half, k)
    width = head_count * HDIM
    rows = [x.reshape(width, length).astype(jnp.bfloat16) for x in (grad_q, grad_k, grad_v)]
    return tuple(lax.all_to_all(x, "seq", split_axis=0, concat_axis=1, tiled=True) for x in rows)


CHIPS = 8
OWN, NEAR, FAR = 0, (1, 2, 3), (4, 5, 6, 7)
ISSUED = (4, 1, 5, 2, 6, 3, 7)
RELAYS = ((0, 1, 2), (3, 4, 5), (6, 7))
TENSORS = 4
VMEM_SPEC = pl.BlockSpec(memory_space=pltpu.VMEM)
PARAMS = pltpu.CompilerParams(vmem_limit_bytes=40 * 1024 * 1024)
SMALL = pl.CostEstimate(flops=1, transcendentals=0, bytes_accessed=1)


def place():
    position = lax.axis_index("seq")
    return position // CORES, position % CORES


def after(x, *others):
    return lax.optimization_barrier((x, *others))[0]


def pack_kernel(flips, *refs):
    ins, outs, sems = refs[:TENSORS], refs[TENSORS:-1], refs[-1]
    chip, _ = place()
    copies = []
    for i, flip in enumerate(flips):
        columns = pl.ds(pl.multiple_of((chip ^ flip) * HDIM, HDIM), HDIM)
        for t in range(TENSORS):
            copies.append(
                pltpu.make_async_copy(ins[t].at[:, columns], outs[i].at[t], sems.at[i, t])
            )
    for copy in copies:
        copy.start()
    for copy in copies:
        copy.wait()


def pack(flips, arrays):
    shape = pltpu.VMEM((TENSORS, arrays[0].shape[0], HDIM), arrays[0].dtype)
    packed = pl.pallas_call(
        functools.partial(pack_kernel, flips),
        out_shape=[shape] * len(flips),
        in_specs=[pl.BlockSpec(memory_space=pl.ANY)] * TENSORS,
        out_specs=[VMEM_SPEC] * len(flips),
        scratch_shapes=[pltpu.SemaphoreType.DMA((len(flips), TENSORS))],
        cost_estimate=SMALL,
    )(*arrays)
    return dict(zip(flips, packed))


def within_blocks(blocks, core, turned, states, grads, intra):
    length = turned.shape[-1]
    half = HDIM // CORES
    own_rows = pl.ds(pl.multiple_of(core * half, half), half)
    row = lax.broadcasted_iota(jnp.int32, (length, length), 0)
    column = lax.broadcasted_iota(jnp.int32, (length, length), 1)
    causal = row >= column
    for i, block in enumerate(blocks):
        q, k, v, g = (block[t] for t in range(TENSORS))
        scores_gv = jnp.where(causal, dot(g, v, NT), 0.0).astype(jnp.bfloat16)
        scores_qk = jnp.where(causal, dot(q, k, NT), 0.0).astype(jnp.bfloat16)
        turned[i, 0] = k.T
        turned[i, 1] = q.T
        turned[i, 2] = g.T
        states[i] = dot(turned[i, 0], v, NN)
        grads[i] = dot(turned[i, 1], g, NN)
        intra[i, 0] = dot(turned[i, 0, own_rows, :], scores_gv, NT)
        intra[i, 1] = dot(turned[i, 1, own_rows, :], scores_gv, NN)
        intra[i, 2] = dot(turned[i, 2, own_rows, :], scores_qk, NN)


def within_shapes(count, length):
    return [
        ((count, HDIM, HDIM), jnp.float32),
        ((count, HDIM, HDIM), jnp.float32),
        ((count, 3, HDIM // CORES, length), jnp.float32),
    ]


def turned_scratch(count, length):
    return pltpu.VMEM((count, 3, HDIM, length), jnp.bfloat16)


def bind(where, refs):
    return [refs[array].at[pl.ds(at * TENSORS, TENSORS)] for array, at in where]


def within_kernel(where, n_arrays, *refs):
    _, core = place()
    within_blocks(bind(where, refs), core, refs[-1], *refs[n_arrays:-1])


def within(where, arrays):
    count, length = len(where), arrays[0].shape[1]
    return pl.pallas_call(
        functools.partial(within_kernel, where, len(arrays)),
        out_shape=[jax.ShapeDtypeStruct(*s) for s in within_shapes(count, length)],
        in_specs=[VMEM_SPEC] * len(arrays),
        out_specs=[VMEM_SPEC] * 3,
        scratch_shapes=[turned_scratch(count, length)],
        cost_estimate=SMALL,
        compiler_params=PARAMS,
    )(*arrays)


def finish_kernel(where, slots, sizes, n_arrays, *refs):
    n_blocks = sum(sizes)
    blocks = bind(where, refs)
    done = [refs[n_arrays + 3 * i : n_arrays + 3 * i + 3] for i in range(len(sizes) - 1)]
    rest = refs[n_arrays + 3 * len(done) :]
    outs, (state_half, grad_half, in_order), last = rest[:3], rest[3:6], rest[6:9]
    turned, ready, sems = rest[9:]
    chip, core = place()
    half, length = HDIM // CORES, turned.shape[-1]
    own_rows = pl.ds(pl.multiple_of(core * half, half), half)
    within_blocks(blocks[n_blocks - sizes[-1] :], core, turned, *last)
    done.append(last)

    found = []
    for size, (states, grads, intra) in zip(sizes, done):
        for i in range(size):
            flip, other = slots[len(found)]
            b = (chip ^ flip) * CORES + (core ^ other)
            in_order[b, 0] = states[i]
            in_order[b, 1] = grads[i]
            found.append((b, intra.at[i]))

    total = jnp.zeros((HDIM, HDIM), jnp.float32)
    for b in range(n_blocks):
        state_half[b] = total.astype(jnp.bfloat16)
        total = total + in_order[b, 0]
    total = jnp.zeros((HDIM, HDIM), jnp.float32)
    for b in reversed(range(n_blocks)):
        rounded = total.astype(jnp.bfloat16)
        grad_half[b, 0] = rounded
        grad_half[b, 1] = rounded.T
        total = total + in_order[b, 1]

    copies = []
    factors = (
        lambda b: state_half[b, own_rows, :],
        lambda b: grad_half[b, 0, own_rows, :],
        lambda b: grad_half[b, 1, own_rows, :],
    )
    for j, (factor, t) in enumerate(zip(factors, (3, 2, 1))):
        for block, (b, intra) in zip(blocks, found):
            columns = pl.ds(pl.multiple_of(b * length, length), length)
            total = intra[j] + dot(factor(b), block[t], NT)
            ready[j, :, columns] = total.astype(ready.dtype)
        copies.append(pltpu.make_async_copy(ready.at[j], outs[j], sems.at[j]))
        copies[-1].start()
    for copy in copies:
        copy.wait()


def finish(where, slots, arrays, sizes, done):
    n_blocks, length = sum(sizes), arrays[0].shape[1]
    out = jax.ShapeDtypeStruct((HDIM // CORES, n_blocks * length), jnp.bfloat16)
    return pl.pallas_call(
        functools.partial(finish_kernel, where, slots, sizes, len(arrays)),
        out_shape=[out] * 3,
        in_specs=[VMEM_SPEC] * (len(arrays) + len(done)),
        out_specs=[pl.BlockSpec(memory_space=pl.ANY)] * 3,
        scratch_shapes=[
            pltpu.VMEM((n_blocks, HDIM, HDIM), jnp.bfloat16),
            pltpu.VMEM((n_blocks, 2, HDIM, HDIM), jnp.bfloat16),
            pltpu.VMEM((n_blocks, 2, HDIM, HDIM), jnp.float32),
        ]
        + [pltpu.VMEM(*s) for s in within_shapes(sizes[-1], length)]
        + [turned_scratch(sizes[-1], length)]
        + [pltpu.VMEM((3,) + out.shape, out.dtype), pltpu.SemaphoreType.DMA((3,))],
        compiler_params=PARAMS,
    )(*arrays, *done)


def chip_body(queries, keys, values, grad_out):
    size = lax.axis_size("seq")
    given = (queries, keys, values, grad_out)
    packed = pack(FAR[:1], given) | pack(FAR[1:] + (OWN,) + NEAR, given)
    flipped = lambda x, flip: lax.ppermute(x, "seq", [(i, i ^ flip) for i in range(size)])
    mine, previous = {OWN: packed[OWN]}, ()
    for flip in ISSUED:
        mine[flip] = after(flipped(packed[flip], flip * CORES), *previous)
        previous = (mine[flip],)

    early = (OWN,) + NEAR + FAR[:-1]
    done = within(tuple((i, 0) for i in range(len(early))), [mine[flip] for flip in early])
    relayed = []
    for flips in RELAYS:
        held = [after(mine[flip], *done) if flips is RELAYS[-1] else mine[flip] for flip in flips]
        relayed.append(flipped(jnp.concatenate(held), 1))
    theirs = [(flip, j, at) for j, flips in enumerate(RELAYS) for at, flip in enumerate(flips)]
    soon, late = theirs[: -len(RELAYS[-1])], theirs[-len(RELAYS[-1]) :]
    beside = tuple((j, at) for _, j, at in soon) + ((len(relayed) - 1, 0),)
    done += within(beside, relayed[:-1] + [mine[FAR[-1]]])

    own = early + FAR[-1:]
    arrays = [mine[flip] for flip in own] + relayed
    where = {(flip, 0): (i, 0) for i, flip in enumerate(own)}
    where |= {(flip, 1): (len(own) + j, at) for flip, j, at in theirs}
    slots = tuple((flip, 0) for flip in early) + tuple((flip, 1) for flip, _, _ in soon)
    slots += ((FAR[-1], 0),) + tuple((flip, 1) for flip, _, _ in late)
    sizes = (len(early), len(beside), len(late))
    return tuple(finish(tuple(where[slot] for slot in slots), slots, arrays, sizes, done))


def solution(mesh):
    in_specs = (P(("groups", "seq"), None),) * 4
    out_specs = (P("seq", "groups"),) * 3

    def body(queries, keys, values, grad_out):
        heads = queries.shape[1] // HDIM
        one_head_per_chip = heads == CHIPS and mesh.shape["seq"] == CHIPS * CORES
        chosen = chip_body if one_head_per_chip else general_body
        return chosen(queries, keys, values, grad_out)

    return jax.shard_map(body, mesh=mesh, in_specs=in_specs, out_specs=out_specs, check_vma=False)
```

```python
import functools

import jax
import jax.numpy as jnp
from jax import lax
from jax.experimental import pallas as pl
from jax.experimental.pallas import tpu as pltpu
from jax.sharding import PartitionSpec as P

HDIM = 128
CORES = 2


def dot(a, b, contract):
    return lax.dot_general(a, b, (contract, ((), ())), preferred_element_type=jnp.float32)


NN = ((1,), (0,))
NT = ((1,), (1,))
TN = ((0,), (0,))


def entering(shard, axis, reverse):
    size, position = lax.axis_size(axis), lax.axis_index(axis)
    everything = lax.all_gather(shard, axis)
    start = jnp.zeros_like(shard)

    def lap(k, before):
        at = size - 1 - k if reverse else k
        reached = at > position if reverse else at < position
        return jnp.where(reached, before + everything[at], before)

    return lax.fori_loop(0, size, lap, start)


def general_body(queries, keys, values, grad_out):
    length = queries.shape[0]
    head_count = queries.shape[1] // HDIM
    split = lambda x: jnp.transpose(x.reshape(length, head_count, HDIM), (1, 0, 2))
    q, k, v, g = split(queries), split(keys), split(values), split(grad_out)
    einsum = functools.partial(jnp.einsum, preferred_element_type=jnp.float32)
    positions = lax.iota(jnp.int32, length)
    causal = positions[:, None] >= positions[None, :]
    scores_qk = jnp.where(causal[None], einsum("htd,hsd->hts", q, k), 0.0).astype(jnp.bfloat16)
    scores_gv = jnp.where(causal[None], einsum("htd,hsd->hts", g, v), 0.0).astype(jnp.bfloat16)
    state_half = entering(einsum("hsd,hse->hde", k, v), "seq", False).astype(jnp.bfloat16)
    grad_half = entering(einsum("htf,htb->hfb", q, g), "seq", True).astype(jnp.bfloat16)
    grad_q = einsum("hsd,hts->hdt", k, scores_gv) + einsum("hdv,htv->hdt", state_half, g)
    grad_k = einsum("htd,hts->hds", q, scores_gv) + einsum("hdv,hsv->hds", grad_half, v)
    grad_v = einsum("htd,hts->hds", g, scores_qk) + einsum("hfb,hsf->hbs", grad_half, k)
    width = head_count * HDIM
    rows = [x.reshape(width, length).astype(jnp.bfloat16) for x in (grad_q, grad_k, grad_v)]
    return tuple(lax.all_to_all(x, "seq", split_axis=0, concat_axis=1, tiled=True) for x in rows)


CHIPS = 8
OWN, NEAR, FAR = 0, (1, 2, 3), (4, 5, 7, 6)
ISSUED = (4, 1, 5, 2, 7, 3, 6)
RELAYS = ((0, 1, 2), (3, 4, 5), (7, 6))
TENSORS = 4
VMEM_SPEC = pl.BlockSpec(memory_space=pltpu.VMEM)
PARAMS = pltpu.CompilerParams(vmem_limit_bytes=40 * 1024 * 1024)
SMALL = pl.CostEstimate(flops=1, transcendentals=0, bytes_accessed=1)


def place():
    position = lax.axis_index("seq")
    return position // CORES, position % CORES


def after(x, *others):
    return lax.optimization_barrier((x, *others))[0]


def pack_kernel(flips, *refs):
    ins, outs, sems = refs[:TENSORS], refs[TENSORS:-1], refs[-1]
    chip, _ = place()
    copies = []
    for i, flip in enumerate(flips):
        columns = pl.ds(pl.multiple_of((chip ^ flip) * HDIM, HDIM), HDIM)
        for t in range(TENSORS):
            copies.append(
                pltpu.make_async_copy(ins[t].at[:, columns], outs[i].at[t], sems.at[i, t])
            )
    for copy in copies:
        copy.start()
    for copy in copies:
        copy.wait()


def pack(flips, arrays):
    shape = pltpu.VMEM((TENSORS, arrays[0].shape[0], HDIM), arrays[0].dtype)
    packed = pl.pallas_call(
        functools.partial(pack_kernel, flips),
        out_shape=[shape] * len(flips),
        in_specs=[pl.BlockSpec(memory_space=pl.ANY)] * TENSORS,
        out_specs=[VMEM_SPEC] * len(flips),
        scratch_shapes=[pltpu.SemaphoreType.DMA((len(flips), TENSORS))],
        cost_estimate=SMALL,
    )(*arrays)
    return dict(zip(flips, packed))


def within_blocks(blocks, core, turned, states, grads, intra):
    length = turned.shape[-1]
    half = HDIM // CORES
    own_rows = pl.ds(pl.multiple_of(core * half, half), half)
    row = lax.broadcasted_iota(jnp.int32, (length, length), 0)
    column = lax.broadcasted_iota(jnp.int32, (length, length), 1)
    causal = row >= column
    masked = lambda x: jnp.where(causal, x, 0.0).astype(jnp.bfloat16)
    scores_gv = [masked(dot(block[3], block[2], NT)) for block in blocks]
    scores_qk = [masked(dot(block[0], block[1], NT)) for block in blocks]
    for i, block in enumerate(blocks):
        for j, t in enumerate((1, 0, 3)):
            turned[i, j] = block[t].T
    for i, block in enumerate(blocks):
        states[i] = dot(turned[i, 0], block[2], NN)
        grads[i] = dot(turned[i, 1], block[3], NN)
    for j, (scores, form) in enumerate(((scores_gv, NT), (scores_gv, NN), (scores_qk, NN))):
        for i in range(len(blocks)):
            intra[i, j] = dot(turned[i, j, own_rows, :], scores[i], form)


def within_shapes(count, length):
    return [
        ((count, HDIM, HDIM), jnp.float32),
        ((count, HDIM, HDIM), jnp.float32),
        ((count, 3, HDIM // CORES, length), jnp.float32),
    ]


def turned_scratch(count, length):
    return pltpu.VMEM((count, 3, HDIM, length), jnp.bfloat16)


def bind(where, refs):
    return [refs[array].at[pl.ds(at * TENSORS, TENSORS)] for array, at in where]


def within_kernel(where, n_arrays, *refs):
    _, core = place()
    within_blocks(bind(where, refs), core, refs[-1], *refs[n_arrays:-1])


def within(where, arrays):
    count, length = len(where), arrays[0].shape[1]
    return pl.pallas_call(
        functools.partial(within_kernel, where, len(arrays)),
        out_shape=[jax.ShapeDtypeStruct(*s) for s in within_shapes(count, length)],
        in_specs=[VMEM_SPEC] * len(arrays),
        out_specs=[VMEM_SPEC] * 3,
        scratch_shapes=[turned_scratch(count, length)],
        cost_estimate=SMALL,
        compiler_params=PARAMS,
    )(*arrays)


def finish_kernel(where, slots, sizes, n_arrays, *refs):
    n_blocks = sum(sizes)
    blocks = bind(where, refs)
    done = [refs[n_arrays + 3 * i : n_arrays + 3 * i + 3] for i in range(len(sizes) - 1)]
    rest = refs[n_arrays + 3 * len(done) :]
    outs, (state_half, grad_half, in_order), last = rest[:3], rest[3:6], rest[6:9]
    turned, ready, sems = rest[9:]
    chip, core = place()
    half, length = HDIM // CORES, turned.shape[-1]
    own_rows = pl.ds(pl.multiple_of(core * half, half), half)
    within_blocks(blocks[n_blocks - sizes[-1] :], core, turned, *last)
    done.append(last)

    found = []
    for size, (states, grads, intra) in zip(sizes, done):
        for i in range(size):
            flip, other = slots[len(found)]
            b = (chip ^ flip) * CORES + (core ^ other)
            in_order[b, 0] = states[i]
            in_order[b, 1] = grads[i]
            found.append((b, intra.at[i]))

    total = jnp.zeros((HDIM, HDIM), jnp.float32)
    for b in range(n_blocks):
        state_half[b] = total.astype(jnp.bfloat16)
        total = total + in_order[b, 0]
    total = jnp.zeros((HDIM, HDIM), jnp.float32)
    for b in reversed(range(n_blocks)):
        rounded = total.astype(jnp.bfloat16)
        grad_half[b, 0] = rounded
        grad_half[b, 1] = rounded.T
        total = total + in_order[b, 1]

    copies = []
    factors = (
        lambda b: state_half[b, own_rows, :],
        lambda b: grad_half[b, 0, own_rows, :],
        lambda b: grad_half[b, 1, own_rows, :],
    )
    for j, (factor, t) in enumerate(zip(factors, (3, 2, 1))):
        for block, (b, intra) in zip(blocks, found):
            columns = pl.ds(pl.multiple_of(b * length, length), length)
            total = intra[j] + dot(factor(b), block[t], NT)
            ready[j, :, columns] = total.astype(ready.dtype)
        copies.append(pltpu.make_async_copy(ready.at[j], outs[j], sems.at[j]))
        copies[-1].start()
    for copy in copies:
        copy.wait()


def finish(where, slots, arrays, sizes, done):
    n_blocks, length = sum(sizes), arrays[0].shape[1]
    out = jax.ShapeDtypeStruct((HDIM // CORES, n_blocks * length), jnp.bfloat16)
    return pl.pallas_call(
        functools.partial(finish_kernel, where, slots, sizes, len(arrays)),
        out_shape=[out] * 3,
        in_specs=[VMEM_SPEC] * (len(arrays) + len(done)),
        out_specs=[pl.BlockSpec(memory_space=pl.ANY)] * 3,
        scratch_shapes=[
            pltpu.VMEM((n_blocks, HDIM, HDIM), jnp.bfloat16),
            pltpu.VMEM((n_blocks, 2, HDIM, HDIM), jnp.bfloat16),
            pltpu.VMEM((n_blocks, 2, HDIM, HDIM), jnp.float32),
        ]
        + [pltpu.VMEM(*s) for s in within_shapes(sizes[-1], length)]
        + [turned_scratch(sizes[-1], length)]
        + [pltpu.VMEM((3,) + out.shape, out.dtype), pltpu.SemaphoreType.DMA((3,))],
        compiler_params=PARAMS,
    )(*arrays, *done)


def chip_body(queries, keys, values, grad_out):
    size = lax.axis_size("seq")
    given = (queries, keys, values, grad_out)
    packed = pack(FAR[:1], given) | pack(FAR[1:] + (OWN,) + NEAR, given)
    flipped = lambda x, flip: lax.ppermute(x, "seq", [(i, i ^ flip) for i in range(size)])
    mine, previous = {OWN: packed[OWN]}, ()
    for flip in ISSUED:
        mine[flip] = after(flipped(packed[flip], flip * CORES), *previous)
        previous = (mine[flip],)

    early = (OWN,) + NEAR + FAR[:-1]
    done = within(tuple((i, 0) for i in range(len(early))), [mine[flip] for flip in early])
    relayed = []
    for flips in RELAYS:
        held = [after(mine[flip], *done) if flips is RELAYS[-1] else mine[flip] for flip in flips]
        relayed.append(flipped(jnp.concatenate(held), 1))
    theirs = [(flip, j, at) for j, flips in enumerate(RELAYS) for at, flip in enumerate(flips)]
    soon, late = theirs[: -len(RELAYS[-1])], theirs[-len(RELAYS[-1]) :]
    beside = tuple((j, at) for _, j, at in soon) + ((len(relayed) - 1, 0),)
    done += within(beside, relayed[:-1] + [mine[FAR[-1]]])

    own = early + FAR[-1:]
    arrays = [mine[flip] for flip in own] + relayed
    where = {(flip, 0): (i, 0) for i, flip in enumerate(own)}
    where |= {(flip, 1): (len(own) + j, at) for flip, j, at in theirs}
    slots = tuple((flip, 0) for flip in early) + tuple((flip, 1) for flip, _, _ in soon)
    slots += ((FAR[-1], 0),) + tuple((flip, 1) for flip, _, _ in late)
    sizes = (len(early), len(beside), len(late))
    return tuple(finish(tuple(where[slot] for slot in slots), slots, arrays, sizes, done))


def solution(mesh):
    in_specs = (P(("groups", "seq"), None),) * 4
    out_specs = (P("seq", "groups"),) * 3

    def body(queries, keys, values, grad_out):
        heads = queries.shape[1] // HDIM
        one_head_per_chip = heads == CHIPS and mesh.shape["seq"] == CHIPS * CORES
        chosen = chip_body if one_head_per_chip else general_body
        return chosen(queries, keys, values, grad_out)

    return jax.shard_map(body, mesh=mesh, in_specs=in_specs, out_specs=out_specs, check_vma=False)
```

```python
import functools

import jax
import jax.numpy as jnp
from jax import lax
from jax.experimental import pallas as pl
from jax.experimental.pallas import tpu as pltpu
from jax.sharding import PartitionSpec as P

HDIM = 128
CORES = 2


def dot(a, b, contract):
    return lax.dot_general(a, b, (contract, ((), ())), preferred_element_type=jnp.float32)


NN = ((1,), (0,))
NT = ((1,), (1,))
TN = ((0,), (0,))


def entering(shard, axis, reverse):
    size, position = lax.axis_size(axis), lax.axis_index(axis)
    everything = lax.all_gather(shard, axis)
    start = jnp.zeros_like(shard)

    def lap(k, before):
        at = size - 1 - k if reverse else k
        reached = at > position if reverse else at < position
        return jnp.where(reached, before + everything[at], before)

    return lax.fori_loop(0, size, lap, start)


def general_body(queries, keys, values, grad_out):
    length = queries.shape[0]
    head_count = queries.shape[1] // HDIM
    split = lambda x: jnp.transpose(x.reshape(length, head_count, HDIM), (1, 0, 2))
    q, k, v, g = split(queries), split(keys), split(values), split(grad_out)
    einsum = functools.partial(jnp.einsum, preferred_element_type=jnp.float32)
    positions = lax.iota(jnp.int32, length)
    causal = positions[:, None] >= positions[None, :]
    scores_qk = jnp.where(causal[None], einsum("htd,hsd->hts", q, k), 0.0).astype(jnp.bfloat16)
    scores_gv = jnp.where(causal[None], einsum("htd,hsd->hts", g, v), 0.0).astype(jnp.bfloat16)
    state_half = entering(einsum("hsd,hse->hde", k, v), "seq", False).astype(jnp.bfloat16)
    grad_half = entering(einsum("htf,htb->hfb", q, g), "seq", True).astype(jnp.bfloat16)
    grad_q = einsum("hsd,hts->hdt", k, scores_gv) + einsum("hdv,htv->hdt", state_half, g)
    grad_k = einsum("htd,hts->hds", q, scores_gv) + einsum("hdv,hsv->hds", grad_half, v)
    grad_v = einsum("htd,hts->hds", g, scores_qk) + einsum("hfb,hsf->hbs", grad_half, k)
    width = head_count * HDIM
    rows = [x.reshape(width, length).astype(jnp.bfloat16) for x in (grad_q, grad_k, grad_v)]
    return tuple(lax.all_to_all(x, "seq", split_axis=0, concat_axis=1, tiled=True) for x in rows)


CHIPS = 8
OWN, NEAR, FAR = 0, (1, 2, 3), (4, 5, 7, 6)
ISSUED = (4, 1, 5, 2, 7, 3, 6)
EARLY = (OWN,) + NEAR + FAR[:-1]
RELAYS = 4
TENSORS = 4
VMEM_SPEC = pl.BlockSpec(memory_space=pltpu.VMEM)
PARAMS = pltpu.CompilerParams(vmem_limit_bytes=40 * 1024 * 1024)
SMALL = pl.CostEstimate(flops=1, transcendentals=0, bytes_accessed=1)


def place():
    position = lax.axis_index("seq")
    return position // CORES, position % CORES


def after(x, *others):
    return lax.optimization_barrier((x, *others))[0]


def pack_kernel(flips, *refs):
    ins, outs, sems = refs[:TENSORS], refs[TENSORS:-1], refs[-1]
    chip, _ = place()
    copies = []
    for i, flip in enumerate(flips):
        columns = pl.ds(pl.multiple_of((chip ^ flip) * HDIM, HDIM), HDIM)
        for t in range(TENSORS):
            copies.append(
                pltpu.make_async_copy(ins[t].at[:, columns], outs[i].at[t], sems.at[i, t])
            )
    for copy in copies:
        copy.start()
    for copy in copies:
        copy.wait()


def pack(flips, arrays):
    shape = pltpu.VMEM((TENSORS, arrays[0].shape[0], HDIM), arrays[0].dtype)
    packed = pl.pallas_call(
        functools.partial(pack_kernel, flips),
        out_shape=[shape] * len(flips),
        in_specs=[pl.BlockSpec(memory_space=pl.ANY)] * TENSORS,
        out_specs=[VMEM_SPEC] * len(flips),
        scratch_shapes=[pltpu.SemaphoreType.DMA((len(flips), TENSORS))],
        cost_estimate=SMALL,
    )(*arrays)
    return dict(zip(flips, packed))


def within_blocks(blocks, core, turned, states, grads, intra):
    length = turned.shape[-1]
    half = HDIM // CORES
    own_rows = pl.ds(pl.multiple_of(core * half, half), half)
    row = lax.broadcasted_iota(jnp.int32, (length, length), 0)
    column = lax.broadcasted_iota(jnp.int32, (length, length), 1)
    causal = row >= column
    masked = lambda x: jnp.where(causal, x, 0.0).astype(jnp.bfloat16)
    scores_gv = [masked(dot(block[3], block[2], NT)) for block in blocks]
    scores_qk = [masked(dot(block[0], block[1], NT)) for block in blocks]
    for i, block in enumerate(blocks):
        for j, t in enumerate((1, 0, 3)):
            turned[i, j] = block[t].T
    for i, block in enumerate(blocks):
        states[i] = dot(turned[i, 0], block[2], NN)
        grads[i] = dot(turned[i, 1], block[3], NN)
    for j, (scores, form) in enumerate(((scores_gv, NT), (scores_gv, NN), (scores_qk, NN))):
        for i in range(len(blocks)):
            intra[i, j] = dot(turned[i, j, own_rows, :], scores[i], form)


def within_shapes(count, length):
    return [
        ((count, HDIM, HDIM), jnp.float32),
        ((count, HDIM, HDIM), jnp.float32),
        ((count, 3, HDIM // CORES, length), jnp.float32),
    ]


def turned_scratch(count, length):
    return pltpu.VMEM((count, 3, HDIM, length), jnp.bfloat16)


class Block:
    def __init__(self, rows):
        self.rows = rows

    def __getitem__(self, t):
        ref, row = self.rows[t]
        return ref[row]


def bind(where, refs):
    return [Block([(refs[array], row) for array, row in rows]) for rows in where]


def within_kernel(where, n_arrays, *refs):
    _, core = place()
    within_blocks(bind(where, refs), core, refs[-1], *refs[n_arrays:-1])


def within(where, arrays):
    count, length = len(where), arrays[0].shape[1]
    return pl.pallas_call(
        functools.partial(within_kernel, where, len(arrays)),
        out_shape=[jax.ShapeDtypeStruct(*s) for s in within_shapes(count, length)],
        in_specs=[VMEM_SPEC] * len(arrays),
        out_specs=[VMEM_SPEC] * 3,
        scratch_shapes=[turned_scratch(count, length)],
        cost_estimate=SMALL,
        compiler_params=PARAMS,
    )(*arrays)


def finish_kernel(where, slots, sizes, n_arrays, *refs):
    n_blocks = sum(sizes)
    blocks = bind(where, refs)
    done = [refs[n_arrays + 3 * i : n_arrays + 3 * i + 3] for i in range(len(sizes) - 1)]
    rest = refs[n_arrays + 3 * len(done) :]
    outs, (state_half, grad_half, in_order), last = rest[:3], rest[3:6], rest[6:9]
    turned, ready, sems = rest[9:]
    chip, core = place()
    half, length = HDIM // CORES, turned.shape[-1]
    own_rows = pl.ds(pl.multiple_of(core * half, half), half)
    within_blocks(blocks[n_blocks - sizes[-1] :], core, turned, *last)
    done.append(last)

    found = []
    for size, (states, grads, intra) in zip(sizes, done):
        for i in range(size):
            flip, other = slots[len(found)]
            b = (chip ^ flip) * CORES + (core ^ other)
            in_order[b, 0] = states[i]
            in_order[b, 1] = grads[i]
            found.append((b, intra.at[i]))

    total = jnp.zeros((HDIM, HDIM), jnp.float32)
    for b in range(n_blocks):
        state_half[b] = total.astype(jnp.bfloat16)
        total = total + in_order[b, 0]
    total = jnp.zeros((HDIM, HDIM), jnp.float32)
    for b in reversed(range(n_blocks)):
        rounded = total.astype(jnp.bfloat16)
        grad_half[b, 0] = rounded
        grad_half[b, 1] = rounded.T
        total = total + in_order[b, 1]

    copies = []
    factors = (
        lambda b: state_half[b, own_rows, :],
        lambda b: grad_half[b, 0, own_rows, :],
        lambda b: grad_half[b, 1, own_rows, :],
    )
    for j, (factor, t) in enumerate(zip(factors, (3, 2, 1))):
        for block, (b, intra) in zip(blocks, found):
            columns = pl.ds(pl.multiple_of(b * length, length), length)
            total = intra[j] + dot(factor(b), block[t], NT)
            ready[j, :, columns] = total.astype(ready.dtype)
        copies.append(pltpu.make_async_copy(ready.at[j], outs[j], sems.at[j]))
        copies[-1].start()
    for copy in copies:
        copy.wait()


def finish(where, slots, arrays, sizes, done):
    n_blocks, length = sum(sizes), arrays[0].shape[1]
    out = jax.ShapeDtypeStruct((HDIM // CORES, n_blocks * length), jnp.bfloat16)
    return pl.pallas_call(
        functools.partial(finish_kernel, where, slots, sizes, len(arrays)),
        out_shape=[out] * 3,
        in_specs=[VMEM_SPEC] * (len(arrays) + len(done)),
        out_specs=[pl.BlockSpec(memory_space=pl.ANY)] * 3,
        scratch_shapes=[
            pltpu.VMEM((n_blocks, HDIM, HDIM), jnp.bfloat16),
            pltpu.VMEM((n_blocks, 2, HDIM, HDIM), jnp.bfloat16),
            pltpu.VMEM((n_blocks, 2, HDIM, HDIM), jnp.float32),
        ]
        + [pltpu.VMEM(*s) for s in within_shapes(sizes[-1], length)]
        + [turned_scratch(sizes[-1], length)]
        + [pltpu.VMEM((3,) + out.shape, out.dtype), pltpu.SemaphoreType.DMA((3,))],
        compiler_params=PARAMS,
    )(*arrays, *done)


def chip_body(queries, keys, values, grad_out):
    size = lax.axis_size("seq")
    given = (queries, keys, values, grad_out)
    packed = pack(FAR[:1], given) | pack(FAR[1:] + (OWN,) + NEAR, given)
    flipped = lambda x, flip: lax.ppermute(x, "seq", [(i, i ^ flip) for i in range(size)])
    mine, previous = {OWN: packed[OWN]}, ()
    for flip in ISSUED:
        mine[flip] = after(flipped(packed[flip], flip * CORES), *previous)
        previous = (mine[flip],)

    rows = [(flip, t) for flip in EARLY for t in range(TENSORS)]
    share = len(rows) // RELAYS
    theirs, relayed = {}, []
    for j in range(RELAYS):
        part = rows[j * share : (j + 1) * share]
        theirs |= {row: (j, at) for at, row in enumerate(part)}
        pieces = [[t for f, t in part if f == flip] for flip in EARLY]
        pieces = [mine[f][ts[0] : ts[-1] + 1] for f, ts in zip(EARLY, pieces) if ts]
        relayed.append(flipped(jnp.concatenate(pieces), 1))

    whole = lambda array: tuple((array, t) for t in range(TENSORS))
    done = within(tuple(whole(i) for i in range(len(EARLY))), [mine[flip] for flip in EARLY])
    last = FAR[-1]
    late = flipped(after(mine[last], *done), 1)
    soon = tuple(tuple(theirs[flip, t] for t in range(TENSORS)) for flip in EARLY)
    done += within(soon + (whole(RELAYS),), relayed + [mine[last]])

    arrays = [mine[flip] for flip in EARLY] + relayed + [mine[last], late]
    shifted = tuple(tuple((len(EARLY) + array, row) for array, row in rows) for rows in soon)
    where = tuple(whole(i) for i in range(len(EARLY))) + shifted
    where += (whole(len(arrays) - 2), whole(len(arrays) - 1))
    slots = tuple((flip, other) for other in range(CORES) for flip in EARLY)
    slots += ((last, 0), (last, 1))
    return tuple(finish(where, slots, arrays, (len(EARLY), len(EARLY) + 1, 1), done))


def solution(mesh):
    in_specs = (P(("groups", "seq"), None),) * 4
    out_specs = (P("seq", "groups"),) * 3

    def body(queries, keys, values, grad_out):
        heads = queries.shape[1] // HDIM
        one_head_per_chip = heads == CHIPS and mesh.shape["seq"] == CHIPS * CORES
        chosen = chip_body if one_head_per_chip else general_body
        return chosen(queries, keys, values, grad_out)

    return jax.shard_map(body, mesh=mesh, in_specs=in_specs, out_specs=out_specs, check_vma=False)
```

```python
import functools

import jax
import jax.numpy as jnp
from jax import lax
from jax.experimental import pallas as pl
from jax.experimental.pallas import tpu as pltpu
from jax.sharding import PartitionSpec as P

HDIM = 128
CORES = 2


def dot(a, b, contract):
    return lax.dot_general(a, b, (contract, ((), ())), preferred_element_type=jnp.float32)


NN = ((1,), (0,))
NT = ((1,), (1,))
TN = ((0,), (0,))


def entering(shard, axis, reverse):
    size, position = lax.axis_size(axis), lax.axis_index(axis)
    everything = lax.all_gather(shard, axis)
    start = jnp.zeros_like(shard)

    def lap(k, before):
        at = size - 1 - k if reverse else k
        reached = at > position if reverse else at < position
        return jnp.where(reached, before + everything[at], before)

    return lax.fori_loop(0, size, lap, start)


def general_body(queries, keys, values, grad_out):
    length = queries.shape[0]
    head_count = queries.shape[1] // HDIM
    split = lambda x: jnp.transpose(x.reshape(length, head_count, HDIM), (1, 0, 2))
    q, k, v, g = split(queries), split(keys), split(values), split(grad_out)
    einsum = functools.partial(jnp.einsum, preferred_element_type=jnp.float32)
    positions = lax.iota(jnp.int32, length)
    causal = positions[:, None] >= positions[None, :]
    scores_qk = jnp.where(causal[None], einsum("htd,hsd->hts", q, k), 0.0).astype(jnp.bfloat16)
    scores_gv = jnp.where(causal[None], einsum("htd,hsd->hts", g, v), 0.0).astype(jnp.bfloat16)
    state_half = entering(einsum("hsd,hse->hde", k, v), "seq", False).astype(jnp.bfloat16)
    grad_half = entering(einsum("htf,htb->hfb", q, g), "seq", True).astype(jnp.bfloat16)
    grad_q = einsum("hsd,hts->hdt", k, scores_gv) + einsum("hdv,htv->hdt", state_half, g)
    grad_k = einsum("htd,hts->hds", q, scores_gv) + einsum("hdv,hsv->hds", grad_half, v)
    grad_v = einsum("htd,hts->hds", g, scores_qk) + einsum("hfb,hsf->hbs", grad_half, k)
    width = head_count * HDIM
    rows = [x.reshape(width, length).astype(jnp.bfloat16) for x in (grad_q, grad_k, grad_v)]
    return tuple(lax.all_to_all(x, "seq", split_axis=0, concat_axis=1, tiled=True) for x in rows)


CHIPS = 8
OWN, NEAR, FAR = 0, (1, 2, 3), (4, 5, 7, 6)
ISSUED = (4, 1, 5, 2, 7, 3, 6)
EARLY = (OWN,) + NEAR + FAR[:-1]
RELAYS = 4
TENSORS = 4
VMEM_SPEC = pl.BlockSpec(memory_space=pltpu.VMEM)
PARAMS = pltpu.CompilerParams(vmem_limit_bytes=40 * 1024 * 1024)
SMALL = pl.CostEstimate(flops=1, transcendentals=0, bytes_accessed=1)


def place():
    position = lax.axis_index("seq")
    return position // CORES, position % CORES


def after(x, *others):
    return lax.optimization_barrier((x, *others))[0]


def pack_kernel(flips, *refs):
    ins, outs, sems = refs[:TENSORS], refs[TENSORS:-1], refs[-1]
    chip, _ = place()
    copies = []
    for i, flip in enumerate(flips):
        columns = pl.ds(pl.multiple_of((chip ^ flip) * HDIM, HDIM), HDIM)
        for t in range(TENSORS):
            copies.append(
                pltpu.make_async_copy(ins[t].at[:, columns], outs[i].at[t], sems.at[i, t])
            )
    for copy in copies:
        copy.start()
    for copy in copies:
        copy.wait()


def pack(flips, arrays):
    shape = pltpu.VMEM((TENSORS, arrays[0].shape[0], HDIM), arrays[0].dtype)
    packed = pl.pallas_call(
        functools.partial(pack_kernel, flips),
        out_shape=[shape] * len(flips),
        in_specs=[pl.BlockSpec(memory_space=pl.ANY)] * TENSORS,
        out_specs=[VMEM_SPEC] * len(flips),
        scratch_shapes=[pltpu.SemaphoreType.DMA((len(flips), TENSORS))],
        cost_estimate=SMALL,
    )(*arrays)
    return dict(zip(flips, packed))


def within_blocks(blocks, core, turned, states, grads, intra, meanwhile=lambda: None):
    length = turned.shape[-1]
    half = HDIM // CORES
    own_rows = pl.ds(pl.multiple_of(core * half, half), half)
    row = lax.broadcasted_iota(jnp.int32, (length, length), 0)
    column = lax.broadcasted_iota(jnp.int32, (length, length), 1)
    causal = row >= column
    masked = lambda x: jnp.where(causal, x, 0.0).astype(jnp.bfloat16)
    scores_gv = [masked(dot(block[3], block[2], NT)) for block in blocks]
    scores_qk = [masked(dot(block[0], block[1], NT)) for block in blocks]
    meanwhile()
    for i, block in enumerate(blocks):
        for j, t in enumerate((1, 0, 3)):
            turned[i, j] = block[t].T
    for i, block in enumerate(blocks):
        states[i] = dot(turned[i, 0], block[2], NN)
        grads[i] = dot(turned[i, 1], block[3], NN)
    for j, (scores, form) in enumerate(((scores_gv, NT), (scores_gv, NN), (scores_qk, NN))):
        for i in range(len(blocks)):
            intra[i, j] = dot(turned[i, j, own_rows, :], scores[i], form)


def within_shapes(count, length):
    return [
        ((count, HDIM, HDIM), jnp.float32),
        ((count, HDIM, HDIM), jnp.float32),
        ((count, 3, HDIM // CORES, length), jnp.float32),
    ]


def turned_scratch(count, length):
    return pltpu.VMEM((count, 3, HDIM, length), jnp.bfloat16)


class Block:
    def __init__(self, rows):
        self.rows = rows

    def __getitem__(self, t):
        ref, row = self.rows[t]
        return ref[row]


def bind(where, refs):
    return [Block([(refs[array], row) for array, row in rows]) for rows in where]


def within_kernel(where, n_arrays, *refs):
    _, core = place()
    within_blocks(bind(where, refs), core, refs[-1], *refs[n_arrays:-1])


def within(where, arrays):
    count, length = len(where), arrays[0].shape[1]
    return pl.pallas_call(
        functools.partial(within_kernel, where, len(arrays)),
        out_shape=[jax.ShapeDtypeStruct(*s) for s in within_shapes(count, length)],
        in_specs=[VMEM_SPEC] * len(arrays),
        out_specs=[VMEM_SPEC] * 3,
        scratch_shapes=[turned_scratch(count, length)],
        cost_estimate=SMALL,
        compiler_params=PARAMS,
    )(*arrays)


def finish_kernel(where, slots, sizes, n_arrays, *refs):
    n_blocks = sum(sizes)
    blocks = bind(where, refs)
    done = [refs[n_arrays + 3 * i : n_arrays + 3 * i + 3] for i in range(len(sizes) - 1)]
    rest = refs[n_arrays + 3 * len(done) :]
    outs, (state_half, grad_half, in_order), last = rest[:3], rest[3:6], rest[6:9]
    turned, ready, sems = rest[9:]
    chip, core = place()
    half, length = HDIM // CORES, turned.shape[-1]
    own_rows = pl.ds(pl.multiple_of(core * half, half), half)
    done.append(last)
    counts = [(states, grads, i) for size, (states, grads, _) in zip(sizes, done) for i in range(size)]
    found = [(chip ^ flip) * CORES + (core ^ other) for flip, other in slots]
    intra = [ref.at[i] for size, (_, _, ref) in zip(sizes, done) for i in range(size)]

    def put(first, end):
        for (states, grads, i), b in list(zip(counts, found))[first:end]:
            in_order[b, 0] = states[i]
            in_order[b, 1] = grads[i]

    early = n_blocks - sizes[-1]
    within_blocks(blocks[early:], core, turned, *last, meanwhile=lambda: put(0, early))
    put(early, n_blocks)

    total = jnp.zeros((HDIM, HDIM), jnp.float32)
    for b in range(n_blocks):
        state_half[b] = total.astype(jnp.bfloat16)
        total = total + in_order[b, 0]

    copies = []

    def product(j, i, factor, t):
        columns = pl.ds(pl.multiple_of(found[i] * length, length), length)
        total = intra[i][j] + dot(factor, blocks[i][t], NT)
        ready[j, :, columns] = total.astype(ready.dtype)

    def leave(j):
        copies.append(pltpu.make_async_copy(ready.at[j], outs[j], sems.at[j]))
        copies[-1].start()

    total = jnp.zeros((HDIM, HDIM), jnp.float32)
    for i in range(n_blocks):
        product(0, i, state_half[found[i], own_rows, :], 3)
        b = n_blocks - 1 - i
        grad_half[b, 0] = total.astype(jnp.bfloat16)
        total = total + in_order[b, 1]
    leave(0)
    for i in range(n_blocks):
        product(1, i, grad_half[found[i], 0, own_rows, :], 2)
        grad_half[i, 1] = grad_half[i, 0].T
    leave(1)
    for i in range(n_blocks):
        product(2, i, grad_half[found[i], 1, own_rows, :], 1)
    leave(2)
    for copy in copies:
        copy.wait()


def finish(where, slots, arrays, sizes, done):
    n_blocks, length = sum(sizes), arrays[0].shape[1]
    out = jax.ShapeDtypeStruct((HDIM // CORES, n_blocks * length), jnp.bfloat16)
    return pl.pallas_call(
        functools.partial(finish_kernel, where, slots, sizes, len(arrays)),
        out_shape=[out] * 3,
        in_specs=[VMEM_SPEC] * (len(arrays) + len(done)),
        out_specs=[pl.BlockSpec(memory_space=pl.ANY)] * 3,
        scratch_shapes=[
            pltpu.VMEM((n_blocks, HDIM, HDIM), jnp.bfloat16),
            pltpu.VMEM((n_blocks, 2, HDIM, HDIM), jnp.bfloat16),
            pltpu.VMEM((n_blocks, 2, HDIM, HDIM), jnp.float32),
        ]
        + [pltpu.VMEM(*s) for s in within_shapes(sizes[-1], length)]
        + [turned_scratch(sizes[-1], length)]
        + [pltpu.VMEM((3,) + out.shape, out.dtype), pltpu.SemaphoreType.DMA((3,))],
        compiler_params=PARAMS,
    )(*arrays, *done)


def chip_body(queries, keys, values, grad_out):
    size = lax.axis_size("seq")
    given = (queries, keys, values, grad_out)
    packed = pack(FAR[:1], given) | pack(FAR[1:] + (OWN,) + NEAR, given)
    flipped = lambda x, flip: lax.ppermute(x, "seq", [(i, i ^ flip) for i in range(size)])
    mine, previous = {OWN: packed[OWN]}, ()
    for flip in ISSUED:
        mine[flip] = after(flipped(packed[flip], flip * CORES), *previous)
        previous = (mine[flip],)

    rows = [(flip, t) for flip in EARLY for t in range(TENSORS)]
    share = len(rows) // RELAYS
    theirs, relayed = {}, []
    for j in range(RELAYS):
        part = rows[j * share : (j + 1) * share]
        theirs |= {row: (j, at) for at, row in enumerate(part)}
        pieces = [[t for f, t in part if f == flip] for flip in EARLY]
        pieces = [mine[f][ts[0] : ts[-1] + 1] for f, ts in zip(EARLY, pieces) if ts]
        relayed.append(flipped(jnp.concatenate(pieces), 1))

    whole = lambda array: tuple((array, t) for t in range(TENSORS))
    done = within(tuple(whole(i) for i in range(len(EARLY))), [mine[flip] for flip in EARLY])
    last = FAR[-1]
    late = flipped(after(mine[last], *done), 1)
    soon = tuple(tuple(theirs[flip, t] for t in range(TENSORS)) for flip in EARLY)
    done += within(soon + (whole(RELAYS),), relayed + [mine[last]])

    arrays = [mine[flip] for flip in EARLY] + relayed + [mine[last], late]
    shifted = tuple(tuple((len(EARLY) + array, row) for array, row in rows) for rows in soon)
    where = tuple(whole(i) for i in range(len(EARLY))) + shifted
    where += (whole(len(arrays) - 2), whole(len(arrays) - 1))
    slots = tuple((flip, other) for other in range(CORES) for flip in EARLY)
    slots += ((last, 0), (last, 1))
    return tuple(finish(where, slots, arrays, (len(EARLY), len(EARLY) + 1, 1), done))


def solution(mesh):
    in_specs = (P(("groups", "seq"), None),) * 4
    out_specs = (P("seq", "groups"),) * 3

    def body(queries, keys, values, grad_out):
        heads = queries.shape[1] // HDIM
        one_head_per_chip = heads == CHIPS and mesh.shape["seq"] == CHIPS * CORES
        chosen = chip_body if one_head_per_chip else general_body
        return chosen(queries, keys, values, grad_out)

    return jax.shard_map(body, mesh=mesh, in_specs=in_specs, out_specs=out_specs, check_vma=False)
```

```python
import functools

import jax
import jax.numpy as jnp
from jax import lax
from jax.experimental import pallas as pl
from jax.experimental.pallas import tpu as pltpu
from jax.sharding import PartitionSpec as P

HDIM = 128
CORES = 2


def dot(a, b, contract):
    return lax.dot_general(a, b, (contract, ((), ())), preferred_element_type=jnp.float32)


NN = ((1,), (0,))
NT = ((1,), (1,))
TN = ((0,), (0,))


def entering(shard, axis, reverse):
    size, position = lax.axis_size(axis), lax.axis_index(axis)
    everything = lax.all_gather(shard, axis)
    start = jnp.zeros_like(shard)

    def lap(k, before):
        at = size - 1 - k if reverse else k
        reached = at > position if reverse else at < position
        return jnp.where(reached, before + everything[at], before)

    return lax.fori_loop(0, size, lap, start)


def general_body(queries, keys, values, grad_out):
    length = queries.shape[0]
    head_count = queries.shape[1] // HDIM
    split = lambda x: jnp.transpose(x.reshape(length, head_count, HDIM), (1, 0, 2))
    q, k, v, g = split(queries), split(keys), split(values), split(grad_out)
    einsum = functools.partial(jnp.einsum, preferred_element_type=jnp.float32)
    positions = lax.iota(jnp.int32, length)
    causal = positions[:, None] >= positions[None, :]
    scores_qk = jnp.where(causal[None], einsum("htd,hsd->hts", q, k), 0.0).astype(jnp.bfloat16)
    scores_gv = jnp.where(causal[None], einsum("htd,hsd->hts", g, v), 0.0).astype(jnp.bfloat16)
    state_half = entering(einsum("hsd,hse->hde", k, v), "seq", False).astype(jnp.bfloat16)
    grad_half = entering(einsum("htf,htb->hfb", q, g), "seq", True).astype(jnp.bfloat16)
    grad_q = einsum("hsd,hts->hdt", k, scores_gv) + einsum("hdv,htv->hdt", state_half, g)
    grad_k = einsum("htd,hts->hds", q, scores_gv) + einsum("hdv,hsv->hds", grad_half, v)
    grad_v = einsum("htd,hts->hds", g, scores_qk) + einsum("hfb,hsf->hbs", grad_half, k)
    width = head_count * HDIM
    rows = [x.reshape(width, length).astype(jnp.bfloat16) for x in (grad_q, grad_k, grad_v)]
    return tuple(lax.all_to_all(x, "seq", split_axis=0, concat_axis=1, tiled=True) for x in rows)


CHIPS = 8
OWN, NEAR, FAR = 0, (1, 2, 3), (4, 5, 7, 6)
ISSUED = (4, 1, 5, 2, 7, 3, 6)
EARLY = (OWN,) + NEAR + FAR[:-1]
RELAYS = 4
TENSORS = 4
VMEM_SPEC = pl.BlockSpec(memory_space=pltpu.VMEM)
PARAMS = pltpu.CompilerParams(vmem_limit_bytes=40 * 1024 * 1024)
SMALL = pl.CostEstimate(flops=1, transcendentals=0, bytes_accessed=1)


def place():
    position = lax.axis_index("seq")
    return position // CORES, position % CORES


def after(x, *others):
    return lax.optimization_barrier((x, *others))[0]


def pack_kernel(flips, *refs):
    ins, outs, sems = refs[:TENSORS], refs[TENSORS:-1], refs[-1]
    chip, _ = place()
    copies = []
    for i, flip in enumerate(flips):
        columns = pl.ds(pl.multiple_of((chip ^ flip) * HDIM, HDIM), HDIM)
        for t in range(TENSORS):
            copies.append(
                pltpu.make_async_copy(ins[t].at[:, columns], outs[i].at[t], sems.at[i, t])
            )
    for copy in copies:
        copy.start()
    for copy in copies:
        copy.wait()


def pack(flips, arrays):
    shape = pltpu.VMEM((TENSORS, arrays[0].shape[0], HDIM), arrays[0].dtype)
    packed = pl.pallas_call(
        functools.partial(pack_kernel, flips),
        out_shape=[shape] * len(flips),
        in_specs=[pl.BlockSpec(memory_space=pl.ANY)] * TENSORS,
        out_specs=[VMEM_SPEC] * len(flips),
        scratch_shapes=[pltpu.SemaphoreType.DMA((len(flips), TENSORS))],
        cost_estimate=SMALL,
    )(*arrays)
    return dict(zip(flips, packed))


def setting(core, length):
    half = HDIM // CORES
    own_rows = pl.ds(pl.multiple_of(core * half, half), half)
    row = lax.broadcasted_iota(jnp.int32, (length, length), 0)
    column = lax.broadcasted_iota(jnp.int32, (length, length), 1)
    return own_rows, lambda x: jnp.where(row >= column, x, 0.0).astype(jnp.bfloat16)


def within_blocks(blocks, core, turned, states, grads, intra):
    own_rows, masked = setting(core, turned.shape[-1])
    scores_gv, scores_qk = [], []
    for i, block in enumerate(blocks):
        for j, t in enumerate((1, 0, 3)):
            turned[i, j] = block[t].T
        scores_gv.append(masked(dot(block[3], block[2], NT)))
    for i, block in enumerate(blocks):
        scores_qk.append(masked(dot(block[0], block[1], NT)))
        intra[i, 0] = dot(turned[i, 0, own_rows, :], scores_gv[i], NT)
        intra[i, 1] = dot(turned[i, 1, own_rows, :], scores_gv[i], NN)
    for i, block in enumerate(blocks):
        states[i] = dot(turned[i, 0], block[2], NN)
        grads[i] = dot(turned[i, 1], block[3], NN)
        intra[i, 2] = dot(turned[i, 2, own_rows, :], scores_qk[i], NN)


def within_last(blocks, core, turned, states, grads, intra, meanwhile):
    own_rows, masked = setting(core, turned.shape[-1])
    scores_gv = [masked(dot(block[3], block[2], NT)) for block in blocks]
    scores_qk = [masked(dot(block[0], block[1], NT)) for block in blocks]
    meanwhile()
    for i, block in enumerate(blocks):
        for j, t in enumerate((1, 0, 3)):
            turned[i, j] = block[t].T
    for i, block in enumerate(blocks):
        states[i] = dot(turned[i, 0], block[2], NN)
        grads[i] = dot(turned[i, 1], block[3], NN)
    for j, (scores, form) in enumerate(((scores_gv, NT), (scores_gv, NN), (scores_qk, NN))):
        for i in range(len(blocks)):
            intra[i, j] = dot(turned[i, j, own_rows, :], scores[i], form)


def within_shapes(count, length):
    return [
        ((count, HDIM, HDIM), jnp.float32),
        ((count, HDIM, HDIM), jnp.float32),
        ((count, 3, HDIM // CORES, length), jnp.float32),
    ]


def turned_scratch(count, length):
    return pltpu.VMEM((count, 3, HDIM, length), jnp.bfloat16)


class Block:
    def __init__(self, rows):
        self.rows = rows

    def __getitem__(self, t):
        ref, row = self.rows[t]
        return ref[row]


def bind(where, refs):
    return [Block([(refs[array], row) for array, row in rows]) for rows in where]


def within_kernel(where, n_arrays, *refs):
    _, core = place()
    within_blocks(bind(where, refs), core, refs[-1], *refs[n_arrays:-1])


def within(where, arrays):
    count, length = len(where), arrays[0].shape[1]
    return pl.pallas_call(
        functools.partial(within_kernel, where, len(arrays)),
        out_shape=[jax.ShapeDtypeStruct(*s) for s in within_shapes(count, length)],
        in_specs=[VMEM_SPEC] * len(arrays),
        out_specs=[VMEM_SPEC] * 3,
        scratch_shapes=[turned_scratch(count, length)],
        cost_estimate=SMALL,
        compiler_params=PARAMS,
    )(*arrays)


def finish_kernel(where, slots, sizes, n_arrays, *refs):
    n_blocks = sum(sizes)
    blocks = bind(where, refs)
    done = [refs[n_arrays + 3 * i : n_arrays + 3 * i + 3] for i in range(len(sizes) - 1)]
    rest = refs[n_arrays + 3 * len(done) :]
    outs, (state_half, grad_half, in_order), last = rest[:3], rest[3:6], rest[6:9]
    turned, ready, sems = rest[9:]
    chip, core = place()
    half, length = HDIM // CORES, turned.shape[-1]
    own_rows = pl.ds(pl.multiple_of(core * half, half), half)
    done.append(last)
    counts = [(states, grads, i) for size, (states, grads, _) in zip(sizes, done) for i in range(size)]
    found = [(chip ^ flip) * CORES + (core ^ other) for flip, other in slots]
    intra = [ref.at[i] for size, (_, _, ref) in zip(sizes, done) for i in range(size)]

    def put(first, end):
        for (states, grads, i), b in list(zip(counts, found))[first:end]:
            in_order[b, 0] = states[i]
            in_order[b, 1] = grads[i]

    early = n_blocks - sizes[-1]
    within_last(blocks[early:], core, turned, *last, meanwhile=lambda: put(0, early))
    put(early, n_blocks)

    total = jnp.zeros((HDIM, HDIM), jnp.float32)
    for b in range(n_blocks):
        state_half[b] = total.astype(jnp.bfloat16)
        total = total + in_order[b, 0]

    copies = []

    def product(j, i, factor, t):
        columns = pl.ds(pl.multiple_of(found[i] * length, length), length)
        total = intra[i][j] + dot(factor, blocks[i][t], NT)
        ready[j, :, columns] = total.astype(ready.dtype)

    def leave(j):
        copies.append(pltpu.make_async_copy(ready.at[j], outs[j], sems.at[j]))
        copies[-1].start()

    total = jnp.zeros((HDIM, HDIM), jnp.float32)
    for i in range(n_blocks):
        product(0, i, state_half[found[i], own_rows, :], 3)
        b = n_blocks - 1 - i
        grad_half[b, 0] = total.astype(jnp.bfloat16)
        total = total + in_order[b, 1]
    leave(0)
    for i in range(n_blocks):
        product(1, i, grad_half[found[i], 0, own_rows, :], 2)
        grad_half[i, 1] = grad_half[i, 0].T
    leave(1)
    for i in range(n_blocks):
        product(2, i, grad_half[found[i], 1, own_rows, :], 1)
    leave(2)
    for copy in copies:
        copy.wait()


def finish(where, slots, arrays, sizes, done):
    n_blocks, length = sum(sizes), arrays[0].shape[1]
    out = jax.ShapeDtypeStruct((HDIM // CORES, n_blocks * length), jnp.bfloat16)
    return pl.pallas_call(
        functools.partial(finish_kernel, where, slots, sizes, len(arrays)),
        out_shape=[out] * 3,
        in_specs=[VMEM_SPEC] * (len(arrays) + len(done)),
        out_specs=[pl.BlockSpec(memory_space=pl.ANY)] * 3,
        scratch_shapes=[
            pltpu.VMEM((n_blocks, HDIM, HDIM), jnp.bfloat16),
            pltpu.VMEM((n_blocks, 2, HDIM, HDIM), jnp.bfloat16),
            pltpu.VMEM((n_blocks, 2, HDIM, HDIM), jnp.float32),
        ]
        + [pltpu.VMEM(*s) for s in within_shapes(sizes[-1], length)]
        + [turned_scratch(sizes[-1], length)]
        + [pltpu.VMEM((3,) + out.shape, out.dtype), pltpu.SemaphoreType.DMA((3,))],
        compiler_params=PARAMS,
    )(*arrays, *done)


def chip_body(queries, keys, values, grad_out):
    size = lax.axis_size("seq")
    given = (queries, keys, values, grad_out)
    packed = pack(FAR[:1], given) | pack(FAR[1:] + (OWN,) + NEAR, given)
    flipped = lambda x, flip: lax.ppermute(x, "seq", [(i, i ^ flip) for i in range(size)])
    mine, previous = {OWN: packed[OWN]}, ()
    for flip in ISSUED:
        mine[flip] = after(flipped(packed[flip], flip * CORES), *previous)
        previous = (mine[flip],)

    rows = [(flip, t) for flip in EARLY for t in range(TENSORS)]
    share = len(rows) // RELAYS
    theirs, relayed = {}, []
    for j in range(RELAYS):
        part = rows[j * share : (j + 1) * share]
        theirs |= {row: (j, at) for at, row in enumerate(part)}
        pieces = [[t for f, t in part if f == flip] for flip in EARLY]
        pieces = [mine[f][ts[0] : ts[-1] + 1] for f, ts in zip(EARLY, pieces) if ts]
        relayed.append(flipped(jnp.concatenate(pieces), 1))

    whole = lambda array: tuple((array, t) for t in range(TENSORS))
    done = within(tuple(whole(i) for i in range(len(EARLY))), [mine[flip] for flip in EARLY])
    last = FAR[-1]
    late = flipped(after(mine[last], *done), 1)
    soon = tuple(tuple(theirs[flip, t] for t in range(TENSORS)) for flip in EARLY)
    done += within(soon + (whole(RELAYS),), relayed + [mine[last]])

    arrays = [mine[flip] for flip in EARLY] + relayed + [mine[last], late]
    shifted = tuple(tuple((len(EARLY) + array, row) for array, row in rows) for rows in soon)
    where = tuple(whole(i) for i in range(len(EARLY))) + shifted
    where += (whole(len(arrays) - 2), whole(len(arrays) - 1))
    slots = tuple((flip, other) for other in range(CORES) for flip in EARLY)
    slots += ((last, 0), (last, 1))
    return tuple(finish(where, slots, arrays, (len(EARLY), len(EARLY) + 1, 1), done))


def solution(mesh):
    in_specs = (P(("groups", "seq"), None),) * 4
    out_specs = (P("seq", "groups"),) * 3

    def body(queries, keys, values, grad_out):
        heads = queries.shape[1] // HDIM
        one_head_per_chip = heads == CHIPS and mesh.shape["seq"] == CHIPS * CORES
        chosen = chip_body if one_head_per_chip else general_body
        return chosen(queries, keys, values, grad_out)

    return jax.shard_map(body, mesh=mesh, in_specs=in_specs, out_specs=out_specs, check_vma=False)
```

```python
import functools

import jax
import jax.numpy as jnp
from jax import lax
from jax.experimental import pallas as pl
from jax.experimental.pallas import tpu as pltpu
from jax.sharding import PartitionSpec as P

HDIM = 128
CORES = 2


def dot(a, b, contract):
    return lax.dot_general(a, b, (contract, ((), ())), preferred_element_type=jnp.float32)


NN = ((1,), (0,))
NT = ((1,), (1,))
TN = ((0,), (0,))


def entering(shard, axis, reverse):
    size, position = lax.axis_size(axis), lax.axis_index(axis)
    everything = lax.all_gather(shard, axis)
    start = jnp.zeros_like(shard)

    def lap(k, before):
        at = size - 1 - k if reverse else k
        reached = at > position if reverse else at < position
        return jnp.where(reached, before + everything[at], before)

    return lax.fori_loop(0, size, lap, start)


def general_body(queries, keys, values, grad_out):
    length = queries.shape[0]
    head_count = queries.shape[1] // HDIM
    split = lambda x: jnp.transpose(x.reshape(length, head_count, HDIM), (1, 0, 2))
    q, k, v, g = split(queries), split(keys), split(values), split(grad_out)
    einsum = functools.partial(jnp.einsum, preferred_element_type=jnp.float32)
    positions = lax.iota(jnp.int32, length)
    causal = positions[:, None] >= positions[None, :]
    scores_qk = jnp.where(causal[None], einsum("htd,hsd->hts", q, k), 0.0).astype(jnp.bfloat16)
    scores_gv = jnp.where(causal[None], einsum("htd,hsd->hts", g, v), 0.0).astype(jnp.bfloat16)
    state_half = entering(einsum("hsd,hse->hde", k, v), "seq", False).astype(jnp.bfloat16)
    grad_half = entering(einsum("htf,htb->hfb", q, g), "seq", True).astype(jnp.bfloat16)
    grad_q = einsum("hsd,hts->hdt", k, scores_gv) + einsum("hdv,htv->hdt", state_half, g)
    grad_k = einsum("htd,hts->hds", q, scores_gv) + einsum("hdv,hsv->hds", grad_half, v)
    grad_v = einsum("htd,hts->hds", g, scores_qk) + einsum("hfb,hsf->hbs", grad_half, k)
    width = head_count * HDIM
    rows = [x.reshape(width, length).astype(jnp.bfloat16) for x in (grad_q, grad_k, grad_v)]
    return tuple(lax.all_to_all(x, "seq", split_axis=0, concat_axis=1, tiled=True) for x in rows)


CHIPS = 8
OWN, NEAR, FAR = 0, (2, 3, 1), (4, 5, 7, 6)
ISSUED = (4, 2, 5, 3, 7, 1, 6)
EARLY = (OWN,) + NEAR + FAR[:-1]
RELAYS = 4
TENSORS = 4
VMEM_SPEC = pl.BlockSpec(memory_space=pltpu.VMEM)
PARAMS = pltpu.CompilerParams(vmem_limit_bytes=40 * 1024 * 1024)
SMALL = pl.CostEstimate(flops=1, transcendentals=0, bytes_accessed=1)


def place():
    position = lax.axis_index("seq")
    return position // CORES, position % CORES


def after(x, *others):
    return lax.optimization_barrier((x, *others))[0]


def pack_kernel(flips, *refs):
    ins, outs, sems = refs[:TENSORS], refs[TENSORS:-1], refs[-1]
    chip, _ = place()
    copies = []
    for i, flip in enumerate(flips):
        columns = pl.ds(pl.multiple_of((chip ^ flip) * HDIM, HDIM), HDIM)
        for t in range(TENSORS):
            copies.append(
                pltpu.make_async_copy(ins[t].at[:, columns], outs[i].at[t], sems.at[i, t])
            )
    for copy in copies:
        copy.start()
    for copy in copies:
        copy.wait()


def pack(flips, arrays):
    shape = pltpu.VMEM((TENSORS, arrays[0].shape[0], HDIM), arrays[0].dtype)
    packed = pl.pallas_call(
        functools.partial(pack_kernel, flips),
        out_shape=[shape] * len(flips),
        in_specs=[pl.BlockSpec(memory_space=pl.ANY)] * TENSORS,
        out_specs=[VMEM_SPEC] * len(flips),
        scratch_shapes=[pltpu.SemaphoreType.DMA((len(flips), TENSORS))],
        cost_estimate=SMALL,
    )(*arrays)
    return dict(zip(flips, packed))


def setting(core, length):
    half = HDIM // CORES
    own_rows = pl.ds(pl.multiple_of(core * half, half), half)
    row = lax.broadcasted_iota(jnp.int32, (length, length), 0)
    column = lax.broadcasted_iota(jnp.int32, (length, length), 1)
    return own_rows, lambda x: jnp.where(row >= column, x, 0.0).astype(jnp.bfloat16)


def within_blocks(blocks, core, turned, states, grads, intra):
    own_rows, masked = setting(core, turned.shape[-1])
    scores_gv, scores_qk = [], []
    for i, block in enumerate(blocks):
        for j, t in enumerate((1, 0, 3)):
            turned[i, j] = block[t].T
        scores_gv.append(masked(dot(block[3], block[2], NT)))
    for i, block in enumerate(blocks):
        scores_qk.append(masked(dot(block[0], block[1], NT)))
        intra[i, 0] = dot(turned[i, 0, own_rows, :], scores_gv[i], NT)
        intra[i, 1] = dot(turned[i, 1, own_rows, :], scores_gv[i], NN)
    for i, block in enumerate(blocks):
        states[i] = dot(turned[i, 0], block[2], NN)
        grads[i] = dot(turned[i, 1], block[3], NN)
        intra[i, 2] = dot(turned[i, 2, own_rows, :], scores_qk[i], NN)


def within_last(blocks, core, turned, states, grads, intra, meanwhile):
    own_rows, masked = setting(core, turned.shape[-1])
    scores_gv = [masked(dot(block[3], block[2], NT)) for block in blocks]
    scores_qk = [masked(dot(block[0], block[1], NT)) for block in blocks]
    meanwhile()
    for i, block in enumerate(blocks):
        for j, t in enumerate((1, 0, 3)):
            turned[i, j] = block[t].T
    for i, block in enumerate(blocks):
        states[i] = dot(turned[i, 0], block[2], NN)
        grads[i] = dot(turned[i, 1], block[3], NN)
    for j, (scores, form) in enumerate(((scores_gv, NT), (scores_gv, NN), (scores_qk, NN))):
        for i in range(len(blocks)):
            intra[i, j] = dot(turned[i, j, own_rows, :], scores[i], form)


def within_shapes(count, length):
    return [
        ((count, HDIM, HDIM), jnp.float32),
        ((count, HDIM, HDIM), jnp.float32),
        ((count, 3, HDIM // CORES, length), jnp.float32),
    ]


def turned_scratch(count, length):
    return pltpu.VMEM((count, 3, HDIM, length), jnp.bfloat16)


class Block:
    def __init__(self, rows):
        self.rows = rows

    def __getitem__(self, t):
        ref, row = self.rows[t]
        return ref[row]


def bind(where, refs):
    return [Block([(refs[array], row) for array, row in rows]) for rows in where]


def within_kernel(where, n_arrays, *refs):
    _, core = place()
    within_blocks(bind(where, refs), core, refs[-1], *refs[n_arrays:-1])


def within(where, arrays):
    count, length = len(where), arrays[0].shape[1]
    return pl.pallas_call(
        functools.partial(within_kernel, where, len(arrays)),
        out_shape=[jax.ShapeDtypeStruct(*s) for s in within_shapes(count, length)],
        in_specs=[VMEM_SPEC] * len(arrays),
        out_specs=[VMEM_SPEC] * 3,
        scratch_shapes=[turned_scratch(count, length)],
        cost_estimate=SMALL,
        compiler_params=PARAMS,
    )(*arrays)


def finish_kernel(where, slots, sizes, n_arrays, *refs):
    n_blocks = sum(sizes)
    blocks = bind(where, refs)
    done = [refs[n_arrays + 3 * i : n_arrays + 3 * i + 3] for i in range(len(sizes) - 1)]
    rest = refs[n_arrays + 3 * len(done) :]
    outs, (state_half, grad_half, in_order), last = rest[:3], rest[3:6], rest[6:9]
    turned, ready, sems = rest[9:]
    chip, core = place()
    half, length = HDIM // CORES, turned.shape[-1]
    own_rows = pl.ds(pl.multiple_of(core * half, half), half)
    done.append(last)
    counts = [(states, grads, i) for size, (states, grads, _) in zip(sizes, done) for i in range(size)]
    found = [(chip ^ flip) * CORES + (core ^ other) for flip, other in slots]
    intra = [ref.at[i] for size, (_, _, ref) in zip(sizes, done) for i in range(size)]

    def put(first, end):
        for (states, grads, i), b in list(zip(counts, found))[first:end]:
            in_order[b, 0] = states[i]
            in_order[b, 1] = grads[i]

    early = n_blocks - sizes[-1]
    within_last(blocks[early:], core, turned, *last, meanwhile=lambda: put(0, early))
    put(early, n_blocks)

    total = jnp.zeros((HDIM, HDIM), jnp.float32)
    for b in range(n_blocks):
        state_half[b] = total.astype(jnp.bfloat16)
        total = total + in_order[b, 0]

    copies = []

    def product(j, i, factor, t):
        columns = pl.ds(pl.multiple_of(found[i] * length, length), length)
        total = intra[i][j] + dot(factor, blocks[i][t], NT)
        ready[j, :, columns] = total.astype(ready.dtype)

    def leave(j):
        copies.append(pltpu.make_async_copy(ready.at[j], outs[j], sems.at[j]))
        copies[-1].start()

    total = jnp.zeros((HDIM, HDIM), jnp.float32)
    for i in range(n_blocks):
        product(0, i, state_half[found[i], own_rows, :], 3)
        b = n_blocks - 1 - i
        grad_half[b, 0] = total.astype(jnp.bfloat16)
        total = total + in_order[b, 1]
    leave(0)
    for i in range(n_blocks):
        product(1, i, grad_half[found[i], 0, own_rows, :], 2)
        grad_half[i, 1] = grad_half[i, 0].T
    leave(1)
    for i in range(n_blocks):
        product(2, i, grad_half[found[i], 1, own_rows, :], 1)
        window = (slice(None), pl.ds(pl.multiple_of(found[i] * length, length), length))
        copies.append(
            pltpu.make_async_copy(ready.at[(2,) + window], outs[2].at[window], sems.at[2 + i])
        )
        copies[-1].start()
    for copy in copies:
        copy.wait()


def finish(where, slots, arrays, sizes, done):
    n_blocks, length = sum(sizes), arrays[0].shape[1]
    out = jax.ShapeDtypeStruct((HDIM // CORES, n_blocks * length), jnp.bfloat16)
    return pl.pallas_call(
        functools.partial(finish_kernel, where, slots, sizes, len(arrays)),
        out_shape=[out] * 3,
        in_specs=[VMEM_SPEC] * (len(arrays) + len(done)),
        out_specs=[pl.BlockSpec(memory_space=pl.ANY)] * 3,
        scratch_shapes=[
            pltpu.VMEM((n_blocks, HDIM, HDIM), jnp.bfloat16),
            pltpu.VMEM((n_blocks, 2, HDIM, HDIM), jnp.bfloat16),
            pltpu.VMEM((n_blocks, 2, HDIM, HDIM), jnp.float32),
        ]
        + [pltpu.VMEM(*s) for s in within_shapes(sizes[-1], length)]
        + [turned_scratch(sizes[-1], length)]
        + [pltpu.VMEM((3,) + out.shape, out.dtype), pltpu.SemaphoreType.DMA((2 + n_blocks,))],
        compiler_params=PARAMS,
    )(*arrays, *done)


def chip_body(queries, keys, values, grad_out):
    size = lax.axis_size("seq")
    given = (queries, keys, values, grad_out)
    packed = pack(FAR[:1], given) | pack(FAR[1:] + (OWN,) + NEAR, given)
    flipped = lambda x, flip: lax.ppermute(x, "seq", [(i, i ^ flip) for i in range(size)])
    mine, previous = {OWN: packed[OWN]}, ()
    for flip in ISSUED:
        mine[flip] = after(flipped(packed[flip], flip * CORES), *previous)
        previous = (mine[flip],)

    rows = [(flip, t) for flip in EARLY for t in range(TENSORS)]
    share = len(rows) // RELAYS
    theirs, relayed = {}, []
    for j in range(RELAYS):
        part = rows[j * share : (j + 1) * share]
        theirs |= {row: (j, at) for at, row in enumerate(part)}
        pieces = [[t for f, t in part if f == flip] for flip in EARLY]
        pieces = [mine[f][ts[0] : ts[-1] + 1] for f, ts in zip(EARLY, pieces) if ts]
        relayed.append(flipped(jnp.concatenate(pieces), 1))

    whole = lambda array: tuple((array, t) for t in range(TENSORS))
    done = within(tuple(whole(i) for i in range(len(EARLY))), [mine[flip] for flip in EARLY])
    last = FAR[-1]
    late = flipped(after(mine[last], *done), 1)
    soon = tuple(tuple(theirs[flip, t] for t in range(TENSORS)) for flip in EARLY)
    done += within(soon + (whole(RELAYS),), relayed + [mine[last]])

    arrays = [mine[flip] for flip in EARLY] + relayed + [mine[last], late]
    shifted = tuple(tuple((len(EARLY) + array, row) for array, row in rows) for rows in soon)
    where = tuple(whole(i) for i in range(len(EARLY))) + shifted
    where += (whole(len(arrays) - 2), whole(len(arrays) - 1))
    slots = tuple((flip, other) for other in range(CORES) for flip in EARLY)
    slots += ((last, 0), (last, 1))
    return tuple(finish(where, slots, arrays, (len(EARLY), len(EARLY) + 1, 1), done))


def solution(mesh):
    in_specs = (P(("groups", "seq"), None),) * 4
    out_specs = (P("seq", "groups"),) * 3

    def body(queries, keys, values, grad_out):
        heads = queries.shape[1] // HDIM
        one_head_per_chip = heads == CHIPS and mesh.shape["seq"] == CHIPS * CORES
        chosen = chip_body if one_head_per_chip else general_body
        return chosen(queries, keys, values, grad_out)

    return jax.shard_map(body, mesh=mesh, in_specs=in_specs, out_specs=out_specs, check_vma=False)
```
